256 devices in a mesh: qb: 8 (over y, core), kb: 16 (over z_lo, x), ba: 2 (over z_hi).
Axes of the slice: x: 4, y: 4, z: 8 (z_hi: 2, z_lo: 4; z = z_hi * 4 + z_lo), core: 2. Of those that a mesh axis runs over, the one named last changes fastest.
Arguments:
- queries: bfloat16 [16384, 1024], P(('ba', 'qb', 'kb')), parts along dimension 0, may hold values from -250 to 250
- keys: bfloat16 [16384, 1024], P(('ba', 'kb')), parts along dimension 0, may hold values from -8 to 8
- values: bfloat16 [16384, 1024], P(('ba', 'kb')), parts along dimension 0, may hold values from -6 to 6
- conv_weight: bfloat16 [8, 6, 11], replicated, may hold values from -0.29882812 to 0.29882812
- mix_weight: float32 [2, 4, 4], replicated, may hold values from -0.2 to 0.2
- doc_ids: int32 [16384], P('ba'), parts along dimension 0, may hold values from 0 to 7, never falling along the last dimension, each value on 1 to 2048 neighbouring positions
Outputs:
- attended: bfloat16 [16384, 1024], P(('ba', 'qb', 'kb')), parts along dimension 0
The draws below stay inside these ranges and needn't reach their ends.
There are 2 independent parts, one for each index of `ba`. The reference program is written for one: setup_inputs(seed, part) draws one part's arguments, and reference() takes and returns one part's arrays. A program takes and returns all parts, laid end to end along the dimension named above; an argument that names none is the same for every part. Nothing has to cross between parts.
All inputs are finite; a program needn't handle non-finite values.
Results may differ from the reference program's by a relative error of at most 0.012.
The reference program's roundings to bfloat16 on the way (of `kernel`, `masked` and `probs`) count: a program that leaves them out, or rounds other values in their place, can miss the bound.
Values may be sent and summed in bfloat16 or wider, within the bound.
A program may use at most 192 MiB of HBM per device.

```python
import math
import jax
import jax.numpy as jnp
import numpy as np
from jax import lax

HEADS = 8
HEAD_DIM = 128
CONV_Q = 6
CONV_K = 11
GROUP = 4
Q_TILE = 1024
SEQ = 8192
N_QB = 8


def draw_pair(key):
    base = jax.random.fold_in(key, 4242)
    key_query, key_key = jax.random.split(base, 2)
    width = HEADS * HEAD_DIM
    query_part = jnp.clip(jax.random.normal(key_query, (SEQ, width), jnp.float32), -6.0, 6.0)
    key_part = jnp.clip(jax.random.normal(key_key, (SEQ, width), jnp.float32), -6.0, 6.0)
    return (query_part, key_part)


def draw_queries(key, part):
    return draw_pair(key)[0].astype(jnp.bfloat16)


def draw_keys(key, part):
    return draw_pair(key)[1].astype(jnp.bfloat16)


def levels(key, dims, cuts, smallest, top_value):
    gain = 1.0
    for dim, parts in cuts:
        steps = jax.random.uniform(jax.random.fold_in(jax.random.fold_in(key, 6), dim), (parts,), jnp.float32, smallest / len(cuts), top_value / len(cuts))
        gain = gain * jnp.repeat(jnp.exp(steps), dims[dim] // parts).reshape((-1,) + (1,) * (len(dims) - 1 - dim))
    return gain


def profile(amount, total, bound, skew):
    loads = [(1 << 20) // math.isqrt(rank ** skew) + 1 for rank in range(2, amount + 1)]
    surplus, given = total - bound - (amount - 1), [1] * (amount - 1)
    while surplus > 0:
        movable = [i for i in range(amount - 1) if given[i] < bound]
        whole, budget = sum([loads[i] for i in movable]), surplus
        for i in movable:
            extra = min(bound - given[i], max(1, budget * loads[i] // whole), surplus)
            given[i] = given[i] + extra
            surplus = surplus - extra
    return np.array([bound] + given)


def ragged_sizes(key, number_of, total, limit, skew):
    if number_of == 2:
        one = jax.random.randint(key, (), max(1, total - limit), min(limit, total - 1) + 1)
        return jnp.stack([one, total - one])
    sizes = jnp.asarray(profile(number_of, total, limit, skew), jnp.int32)
    pairs = (number_of - 1) // 2
    giver, taker = sizes[1:1 + 2 * pairs:2], sizes[2:2 + 2 * pairs:2]
    room = jnp.minimum(giver - 1, limit - taker)
    moved = jax.random.randint(jax.random.fold_in(key, 1), (pairs,), 0, 1 << 20) % (room + 1)
    sizes = sizes.at[1:1 + 2 * pairs:2].set(giver - moved).at[2:2 + 2 * pairs:2].set(taker + moved)
    return sizes[jax.random.permutation(jax.random.fold_in(key, 2), number_of)]


def centred(own_key, extent, scale, bound, cuts=(), kind=jnp.bfloat16):
    values = scale * jax.random.normal(own_key, extent, jnp.float32)
    if cuts:
        values = values * levels(own_key, extent, cuts, -0.22, 0.18)
    return jnp.clip(values, -bound, bound).astype(kind)


def setup_inputs(seed: int = 0, part: int = 0) -> dict:
    seeds = jax.random.split(jax.random.key(seed), 7)
    own_keys = jax.random.split(jax.random.fold_in(seeds[6], part), 7)
    queries = draw_queries(jax.random.fold_in(jax.random.fold_in(seeds[6], part), 71), part)
    keys = draw_keys(jax.random.fold_in(jax.random.fold_in(seeds[6], part), 71), part)
    values = centred(own_keys[2], (SEQ, HEADS * HEAD_DIM), 1.0, 6.0, ((0, 16),))
    conv_weight = jnp.clip(jax.random.uniform(seeds[3], (HEADS, CONV_Q, CONV_K), jnp.float32, -0.29882812, 0.29882812), -0.29882812, 0.29882812).astype(jnp.bfloat16)
    mix_weight = jnp.clip(jax.random.uniform(seeds[4], (HEADS // GROUP, GROUP, GROUP), jnp.float32, -0.2, 0.2), -0.2, 0.2)
    doc_ids = jnp.searchsorted(jnp.cumsum(ragged_sizes(own_keys[5], 8, SEQ, SEQ // 4, 1)), jnp.arange(SEQ), side="right").astype(jnp.int32)
    return {"queries": queries, "keys": keys, "values": values, "conv_weight": conv_weight, "mix_weight": mix_weight, "doc_ids": doc_ids}


def kernel_of(conv_weight):
    reach = conv_weight.shape[2]
    center = (jnp.arange(conv_weight.shape[1])[:, None] == 0) & (jnp.arange(reach)[None, :] == reach // 2)
    return (conv_weight.astype(jnp.float32) + center.astype(jnp.float32)[None]).astype(jnp.bfloat16)

def reference(queries, keys, values, conv_weight, mix_weight, doc_ids):
    rows_above = CONV_Q - 1
    side = CONV_K // 2
    margin = max(rows_above, side)
    width = HEADS * HEAD_DIM
    scale = 1.0 / math.sqrt(HEAD_DIM)
    kernel = kernel_of(conv_weight).astype(jnp.float32)
    flipped = kernel[:, ::-1, ::-1][:, None, :, :]
    mixer = mix_weight.astype(jnp.float32) + jnp.eye(GROUP, dtype=jnp.float32)[None]
    q_pad = jnp.concatenate([jnp.zeros((rows_above, width), jnp.bfloat16), queries], axis=0)
    k_side = jnp.zeros((side, width), jnp.bfloat16)
    k_all = jnp.concatenate([k_side, keys, k_side], axis=0).astype(jnp.float32).reshape(SEQ + 2 * side, HEADS, HEAD_DIM)
    v_all = values.astype(jnp.float32).reshape(SEQ, HEADS, HEAD_DIM)
    fence = jnp.full((margin,), -1, jnp.int32)
    id_pad = jnp.concatenate([fence, doc_ids.astype(jnp.int32), fence])
    col_ids = id_pad[margin - side:margin + SEQ + side]
    col_pos = jnp.arange(SEQ + 2 * side, dtype=jnp.int32) - side

    def block_out(index):
        start = (index * Q_TILE).astype(jnp.int32)
        q_ext = lax.dynamic_slice_in_dim(q_pad, start, Q_TILE + rows_above, 0).astype(jnp.float32)
        q_ext = q_ext.reshape(Q_TILE + rows_above, HEADS, HEAD_DIM)
        logits = jnp.einsum('rhd,chd->hrc', q_ext, k_all) * scale
        row_ids = lax.dynamic_slice_in_dim(id_pad, start + margin - rows_above, Q_TILE + rows_above, 0)
        row_pos = start - rows_above + jnp.arange(Q_TILE + rows_above, dtype=jnp.int32)
        allowed = (row_ids[:, None] == col_ids[None, :]) & (col_ids[None, :] >= 0) & (col_pos[None, :] <= row_pos[:, None])
        masked = jnp.where(allowed[None, :, :], logits, 0.0).astype(jnp.bfloat16)
        masked = lax.optimization_barrier(masked).astype(jnp.float32)
        conv = lax.conv_general_dilated(masked[None], flipped, (1, 1), 'VALID', feature_group_count=HEADS, precision=lax.Precision.HIGHEST)[0]
        grouped = conv.reshape(HEADS // GROUP, GROUP, Q_TILE, SEQ)
        mixed = jnp.einsum('gpq,gqrc->rgpc', mixer, grouped, precision=lax.Precision.HIGHEST).reshape(Q_TILE, HEADS, SEQ)
        own = allowed[rows_above:, side:side + SEQ]
        scores = jnp.where(own[:, None, :], mixed, -jnp.inf)
        row_top = lax.optimization_barrier(jnp.max(scores, axis=2, keepdims=True))
        expo = jnp.exp(scores - row_top)
        weight_sum = lax.optimization_barrier(jnp.sum(expo, axis=2))
        probs = expo.astype(jnp.bfloat16)
        probs = lax.optimization_barrier(probs).astype(jnp.float32)
        summed = jnp.einsum('rhc,chd->rhd', probs, v_all)
        result = summed / weight_sum[:, :, None]
        return result.reshape(Q_TILE, width).astype(jnp.bfloat16)
    blocks = lax.map(block_out, jnp.arange(N_QB, dtype=jnp.int32))
    return blocks.reshape(SEQ, width)
```

```python
import math

import jax
import jax.numpy as jnp
from jax import lax
from jax.experimental import pallas as pl
from jax.experimental.pallas import tpu as pltpu
from jax.sharding import PartitionSpec as P

MESH = pl.DeviceIdType.MESH
F32 = jnp.float32
BF16 = jnp.bfloat16

CHUNK = 64
HALO = 16
EXT = CHUNK + HALO
SPAN = 5
BLOCK = 512
HALF = 256
LANE = 128
LAGS = 6
REACH = 11
SIDE = 5
HEADS = 8
GROUP = 4
GROUPS = 2
DEPTH = LAGS * HALF + LANE
ROWS = SPAN * CHUNK
EROWS = SPAN * EXT
HALFW = GROUP * LANE
LOW = -1e30
WIDTH = HEADS * LANE


def turn(block):
    return 5 - 4 * (block % 2)


def worker(chunk, lag):
    group, place = chunk // 8, chunk % 8
    return (place + 8 - turn(group)) % 8, (group + 16 - lag) % 16


def owner(chunk):
    return chunk // 16, chunk % 16


def served(qb, kb, lag):
    group = (kb + lag) % 16
    return group * 8 + (qb + turn(group)) % 8


def iota(shape, dim):
    return lax.broadcasted_iota(jnp.int32, shape, dim)


def dot_nt(a, b):
    return lax.dot_general(a, b, (((1,), (1,)), ((), ())), preferred_element_type=F32)


def build_masks(qb, kb, doc_ref, msc_ref):
    scale = 1.0 / math.sqrt(LANE)
    docs = doc_ref[...]
    starts = []
    for value in range(1, 8):
        below = (docs < value).astype(F32)
        below = jnp.sum(jnp.sum(below, axis=0, keepdims=True), axis=1, keepdims=True)
        starts.append(jnp.broadcast_to(below.astype(jnp.int32), (EXT, LANE)))
    lane = iota((EXT, LANE), 1)
    first = kb * BLOCK
    edge = lane % 16
    edge = jnp.where(edge < 8, edge - 8, edge + (HALF - 8))
    for lag in range(SPAN):
        row = served(qb, kb, lag) * CHUNK - HALO + iota((EXT, LANE), 0)
        low = jnp.zeros((EXT, LANE), jnp.int32)
        for start in starts:
            low = jnp.where(start <= row, start, low)
        for tile in range(6):
            if tile < 4:
                col = first + tile * LANE + lane
            else:
                col = first + (tile - 4) * HALF + edge
            good = (col >= low) & (col <= row)
            msc_ref[tile, lag * EXT : (lag + 1) * EXT, :] = jnp.where(good, scale, 0.0).astype(F32)


def build_bands(cw_ref, base_ref, w_ref):
    base_ref[...] = jnp.zeros_like(base_ref)
    center = (iota((LAGS, REACH), 0) == 0) & (iota((LAGS, REACH), 1) == REACH // 2)
    for h in range(HEADS):
        taps = cw_ref[h].astype(F32) + center.astype(F32)
        base_ref[8 * h : 8 * h + LAGS, 0:REACH] = taps
    base_ref[...] = pltpu.roll(base_ref[...], LANE - SIDE, 1)
    w_ref[...] = jnp.zeros_like(w_ref)
    diff = iota((LANE, LANE), 1) - iota((LANE, LANE), 0)
    near = (diff <= SIDE) & (diff >= -SIDE)
    blank = jnp.zeros((8, LANE), F32)

    def one_head(h, carry):
        base = base_ref[pl.ds(pl.multiple_of(h * 8, 8), 8), :]
        for a in range(LAGS):
            ring = jnp.broadcast_to(base[a : a + 1, :], (LANE, LANE))
            ring = pltpu.roll(ring, 0, 1, stride=1, stride_axis=0)
            diag = jnp.where(near, ring, 0.0).astype(BF16)
            upper = jnp.where(diff[LANE - 8 :] <= SIDE - LANE, ring[LANE - 8 :], 0.0)
            lower = jnp.where(diff[:8] >= LANE - SIDE, ring[:8], 0.0)
            top = a * HALF
            w_ref[h, top : top + LANE, 0:LANE] = diag
            w_ref[h, top + LANE : top + HALF, LANE:HALF] = diag
            w_ref[h, top + LANE - 16 : top + LANE, LANE:HALF] = jnp.concatenate(
                [blank, upper], axis=0
            ).astype(BF16)
            w_ref[h, top + LANE : top + LANE + 16, 0:LANE] = jnp.concatenate(
                [lower, blank], axis=0
            ).astype(BF16)
            edge = LAGS * HALF + 16 * a
            w_ref[h, edge : edge + 16, 0:LANE] = jnp.concatenate([upper, blank], axis=0).astype(BF16)
            w_ref[h, edge : edge + 16, LANE:HALF] = jnp.concatenate(
                [blank, lower], axis=0
            ).astype(BF16)
        return carry

    lax.fori_loop(0, HEADS, one_head, 0)


def build_edges(k_ref, kn_ref, kt_ref):
    left = [kn_ref[0], k_ref[HALF - 16 : HALF, :]]
    right = [k_ref[HALF : HALF + 16, :], kn_ref[1]]
    for t in range(2):
        pair = jnp.concatenate([left[t].astype(F32)[8:16], right[t].astype(F32)[0:8]], axis=0)
        pair = pair.astype(BF16)
        for a in range(8):
            kt_ref[t * LANE + 16 * a : t * LANE + 16 * a + 16, :] = pair


def attend_group(g, mw_ref, qg_ref, k_ref, v_ref, kt_ref, w_ref, msc_ref, scratch, ob_ref, st_ref):
    msk_ref, x_ref, conv_ref, probs_ref = scratch
    lane = iota((CHUNK, LANE), 1)

    def one_head(p, carry):
        h = g * GROUP + p
        cols = pl.ds(pl.multiple_of(h * LANE, LANE), LANE)
        q = qg_ref[:, cols]
        for t in range(3):
            keys = k_ref[t * HALF : (t + 1) * HALF, cols] if t < 2 else kt_ref[:, cols]
            logits = dot_nt(q, keys)
            for u in range(2):
                msk_ref[2 * t + u] = logits[:, u * LANE : (u + 1) * LANE] * msc_ref[2 * t + u]
        for lag in range(SPAN):
            base = lag * EXT + HALO
            for t in range(2):
                to = t * ROWS + lag * CHUNK
                for a in range(LAGS):
                    for u in range(2):
                        piece = msk_ref[2 * t + u, base - a : base - a + CHUNK, :]
                        at = a * HALF + u * LANE
                        x_ref[to : to + CHUNK, at : at + LANE] = piece.astype(BF16)
                piece = msk_ref[4 + t, base : base + CHUNK, :]
                for a in range(1, LAGS):
                    other = msk_ref[4 + t, base - a : base - a + CHUNK, :]
                    piece = jnp.where(lane >= 16 * a, other, piece)
                x_ref[to : to + CHUNK, LAGS * HALF : DEPTH] = piece.astype(BF16)
        conv_ref[p] = jnp.dot(x_ref[...], w_ref[h], preferred_element_type=F32)
        return carry

    lax.fori_loop(0, GROUP, one_head, 0)
    weights = [
        [mw_ref[g, p, q] + (1.0 if p == q else 0.0) for q in range(GROUP)] for p in range(GROUP)
    ]
    small = iota((16, LANE), 1)

    def soft_rows(b, carry):
        row = pl.multiple_of(b * 16, 16)
        erow = pl.multiple_of((b + b // 4 + 1) * 16, 16)
        good = [msc_ref[tile, pl.ds(erow, 16), :] > 0 for tile in range(4)]
        conv = [
            [
                conv_ref[q, pl.ds(pl.multiple_of((tile // 2) * ROWS + row, 16), 16),
                         (tile % 2) * LANE : (tile % 2 + 1) * LANE]
                for tile in range(4)
            ]
            for q in range(GROUP)
        ]
        stats = jnp.zeros((16, LANE), F32)
        for p in range(GROUP):
            mixed = []
            for tile in range(4):
                total = conv[0][tile] * weights[p][0]
                for q in range(1, GROUP):
                    total = total + conv[q][tile] * weights[p][q]
                mixed.append(jnp.where(good[tile], total, LOW))
            top = jnp.maximum(jnp.maximum(mixed[0], mixed[1]), jnp.maximum(mixed[2], mixed[3]))
            top = jnp.max(top, axis=1, keepdims=True)
            expo = [jnp.exp(m - top) for m in mixed]
            for tile in range(4):
                probs_ref[p, pl.ds(row, 16), tile * LANE : (tile + 1) * LANE] = expo[tile].astype(BF16)
            total = jnp.sum((expo[0] + expo[1]) + (expo[2] + expo[3]), axis=1, keepdims=True)
            stats = jnp.where(small == p, top, stats)
            stats = jnp.where(small == GROUP + p, total, stats)
        st_ref[g, pl.ds(row, 16), :] = stats
        return carry

    lax.fori_loop(0, ROWS // 16, soft_rows, 0)

    def one_out(p, carry):
        cols = pl.ds(pl.multiple_of((g * GROUP + p) * LANE, LANE), LANE)
        out = jnp.dot(probs_ref[p], v_ref[:, cols], preferred_element_type=F32)
        ob_ref[:, cols] = out.astype(BF16)
        return carry

    lax.fori_loop(0, GROUP, one_out, 0)


def combine_group(g, og_ref, sg_ref, out_ref):
    parts = [sg_ref[g, lag] for lag in range(SPAN)]
    top = parts[0]
    for part in parts[1:]:
        top = jnp.maximum(top, part)
    scales = [jnp.exp(part - top) for part in parts]
    total = jnp.zeros((CHUNK, LANE), F32)
    for part, scale in zip(parts, scales):
        total = total + scale * pltpu.roll(part, LANE - GROUP, 1)
    for p in range(GROUP):
        cols = pl.ds(pl.multiple_of((g * GROUP + p) * LANE, LANE), LANE)
        acc = jnp.zeros((CHUNK, LANE), F32)
        for lag in range(SPAN):
            acc = acc + og_ref[lag, :, cols].astype(F32) * scales[lag][:, p : p + 1]
        out_ref[:, cols] = (acc / total[:, p : p + 1]).astype(BF16)


def kernel(
    q_hbm, k_hbm, v_hbm, cw_ref, mw_ref, doc_ref, out_ref,
    qg_ref, k_ref, v_ref, kn_ref, kt_ref, base_ref, w_ref, msc_ref,
    msk_ref, x_ref, conv_ref, probs_ref, ob_ref, st_ref, og_ref, sg_ref,
    local_sem, q_send, q_recv, h_send, h_recv, n_send, n_recv, o_send, o_recv, s_send, s_recv,
):
    qb, kb = lax.axis_index("qb"), lax.axis_index("kb")
    mine = qb * 16 + kb
    after = (mine + 1) % 128
    place = lambda where: {"qb": where[0], "kb": where[1]}
    below, above = (kb + 1) % 16, (kb + 15) % 16

    load_k = pltpu.make_async_copy(k_hbm, k_ref, local_sem.at[0])
    load_v = pltpu.make_async_copy(v_hbm, v_ref, local_sem.at[1])
    load_k.start()
    load_v.start()

    barrier = pltpu.get_barrier_semaphore()
    peers = [place((qb, below)), place((qb, above))]
    for lag in range(SPAN):
        took = served(qb, kb, lag)
        peers.append(place(worker(mine, lag)))
        peers.append(place(worker(after, lag)))
        peers.append(place(owner(took)))
        peers.append(place(owner((took + 127) % 128)))
    for peer in peers:
        pl.semaphore_signal(barrier, inc=1, device_id=peer, device_id_type=MESH)
    pl.semaphore_wait(barrier, len(peers))

    def remote(src, dst, send, recv, where):
        return pltpu.make_async_remote_copy(
            src_ref=src, dst_ref=dst, send_sem=send, recv_sem=recv,
            device_id=where, device_id_type=MESH,
        )

    def chunk_copy(g, lag):
        cols = pl.ds(pl.multiple_of(g * HALFW, HALFW), HALFW)
        return remote(
            q_hbm.at[:, cols], qg_ref.at[lag * EXT + HALO : (lag + 1) * EXT, cols],
            q_send.at[g, lag], q_recv.at[g, lag], place(worker(mine, lag)),
        )

    def halo_copy(g, lag):
        cols = pl.ds(pl.multiple_of(g * HALFW, HALFW), HALFW)
        return remote(
            q_hbm.at[CHUNK - HALO : CHUNK, cols], qg_ref.at[lag * EXT : lag * EXT + HALO, cols],
            h_send.at[g, lag], h_recv.at[g, lag], place(worker(after, lag)),
        )

    def out_copy(g, lag):
        cols = pl.ds(pl.multiple_of(g * HALFW, HALFW), HALFW)
        return remote(
            ob_ref.at[lag * CHUNK : (lag + 1) * CHUNK, cols], og_ref.at[lag, :, cols],
            o_send.at[g, lag], o_recv.at[g, lag], place(owner(served(qb, kb, lag))),
        )

    def stat_copy(g, lag):
        return remote(
            st_ref.at[g, lag * CHUNK : (lag + 1) * CHUNK, :], sg_ref.at[g, lag],
            s_send.at[g, lag], s_recv.at[g, lag], place(owner(served(qb, kb, lag))),
        )

    edge_copies = [
        remote(k_hbm.at[BLOCK - 16 : BLOCK, :], kn_ref.at[0], n_send.at[0], n_recv.at[0],
               place((qb, below))),
        remote(k_hbm.at[0:16, :], kn_ref.at[1], n_send.at[1], n_recv.at[1], place((qb, above))),
    ]
    for copy in edge_copies:
        copy.start()
    for g in range(GROUPS):
        for lag in range(SPAN):
            halo_copy(g, lag).start()
            chunk_copy(g, lag).start()

    build_masks(qb, kb, doc_ref, msc_ref)
    build_bands(cw_ref, base_ref, w_ref)
    load_k.wait()
    for copy in edge_copies:
        copy.wait()
    build_edges(k_ref, kn_ref, kt_ref)
    load_v.wait()

    def one_group(g, carry):
        for lag in range(SPAN):
            halo_copy(g, lag).wait()
            chunk_copy(g, lag).wait()
        attend_group(
            g, mw_ref, qg_ref, k_ref, v_ref, kt_ref, w_ref, msc_ref,
            (msk_ref, x_ref, conv_ref, probs_ref), ob_ref, st_ref,
        )
        for lag in range(SPAN):
            out_copy(g, lag).start()
            stat_copy(g, lag).start()
        return carry

    lax.fori_loop(0, GROUPS, one_group, 0)

    def one_result(g, carry):
        for lag in range(SPAN):
            out_copy(g, lag).wait()
            stat_copy(g, lag).wait()
        combine_group(g, og_ref, sg_ref, out_ref)
        return carry

    lax.fori_loop(0, GROUPS, one_result, 0)


def body(queries, keys, values, conv_weight, mix_weight, doc_ids):
    docs = doc_ids.reshape(-1, LANE)
    any_space = pl.BlockSpec(memory_space=pl.ANY)
    vmem = pl.BlockSpec(memory_space=pltpu.VMEM)
    dma = pltpu.SemaphoreType.DMA
    return pl.pallas_call(
        kernel,
        out_shape=jax.ShapeDtypeStruct((CHUNK, WIDTH), BF16),
        in_specs=[
            any_space, any_space, any_space, vmem, pl.BlockSpec(memory_space=pltpu.SMEM), vmem,
        ],
        out_specs=vmem,
        scratch_shapes=[
            pltpu.VMEM((EROWS, WIDTH), BF16),
            pltpu.VMEM((BLOCK, WIDTH), BF16),
            pltpu.VMEM((BLOCK, WIDTH), BF16),
            pltpu.VMEM((2, 16, WIDTH), BF16),
            pltpu.VMEM((2 * LANE, WIDTH), BF16),
            pltpu.VMEM((8 * HEADS, LANE), F32),
            pltpu.VMEM((HEADS, DEPTH, HALF), BF16),
            pltpu.VMEM((6, EROWS, LANE), F32),
            pltpu.VMEM((6, EROWS, LANE), F32),
            pltpu.VMEM((2 * ROWS, DEPTH), BF16),
            pltpu.VMEM((GROUP, 2 * ROWS, HALF), F32),
            pltpu.VMEM((GROUP, ROWS, BLOCK), BF16),
            pltpu.VMEM((ROWS, WIDTH), BF16),
            pltpu.VMEM((GROUPS, ROWS, LANE), F32),
            pltpu.VMEM((SPAN, CHUNK, WIDTH), BF16),
            pltpu.VMEM((GROUPS, SPAN, CHUNK, LANE), F32),
            dma((2,)),
            dma((GROUPS, SPAN)), dma((GROUPS, SPAN)),
            dma((GROUPS, SPAN)), dma((GROUPS, SPAN)),
            dma((2,)), dma((2,)),
            dma((GROUPS, SPAN)), dma((GROUPS, SPAN)),
            dma((GROUPS, SPAN)), dma((GROUPS, SPAN)),
        ],
        compiler_params=pltpu.CompilerParams(collective_id=0, has_side_effects=True),
    )(queries, keys, values, conv_weight, mix_weight, docs)


def solution(mesh):
    placed = (
        P(("ba", "qb", "kb"), None),
        P(("ba", "kb"), None),
        P(("ba", "kb"), None),
        P(),
        P(),
        P("ba"),
    )
    return jax.shard_map(
        body, mesh=mesh, in_specs=placed, out_specs=P(("ba", "qb", "kb"), None), check_vma=False
    )
```

```python
import math

import jax
import jax.numpy as jnp
from jax import lax
from jax.experimental import pallas as pl
from jax.experimental.pallas import tpu as pltpu
from jax.sharding import PartitionSpec as P

MESH = pl.DeviceIdType.MESH
F32 = jnp.float32
BF16 = jnp.bfloat16

CHUNK = 64
HALO = 16
EXT = CHUNK + HALO
TURN = (2, 4)
SPAN = 5
BLOCK = 512
HALF = 256
LANE = 128
LAGS = 6
REACH = 11
SIDE = 5
HEADS = 8
GROUP = 4
GROUPS = 2
DEPTH = LAGS * HALF + LANE
ROWS = SPAN * CHUNK
EROWS = SPAN * EXT
HALFW = GROUP * LANE
LOW = -1e30
WIDTH = HEADS * LANE


def shift(group):
    return 5 * (group // 2) + TURN[0] + (TURN[1] - TURN[0]) * (group % 2)


def column(chunk):
    return (chunk % 8 + 64 - shift(chunk // 8)) % 8


def worker(chunk, lag):
    return column(chunk), chunk // 8 - lag


def joiner(chunk):
    return column(chunk), chunk % 16


def owner(chunk):
    return chunk // 16, chunk % 16


def served(qb, kb, lag):
    group = kb + lag
    return group * 8 + (qb + shift(group)) % 8


def joined(qb, kb):
    turn = TURN[0] + (TURN[1] - TURN[0]) * (kb // 8)
    return (5 * (kb % 8 + 16 - turn - qb)) % 8 * 16 + kb


def iota(shape, dim):
    return lax.broadcasted_iota(jnp.int32, shape, dim)


def dot_nt(a, b):
    return lax.dot_general(a, b, (((1,), (1,)), ((), ())), preferred_element_type=F32)


def build_masks(qb, kb, doc_ref, msc_ref):
    scale = 1.0 / math.sqrt(LANE)
    docs = doc_ref[...]
    starts = []
    for value in range(1, 8):
        below = (docs < value).astype(F32)
        below = jnp.sum(jnp.sum(below, axis=0, keepdims=True), axis=1, keepdims=True)
        starts.append(jnp.broadcast_to(below.astype(jnp.int32), (EXT, LANE)))
    lane = iota((EXT, LANE), 1)
    first = kb * BLOCK
    edge = lane % 16
    edge = jnp.where(edge < 8, edge - 8, edge + (HALF - 8))
    for lag in range(SPAN):
        row = served(qb, kb, lag) * CHUNK - HALO + iota((EXT, LANE), 0)
        low = jnp.zeros((EXT, LANE), jnp.int32)
        for start in starts:
            low = jnp.where(start <= row, start, low)
        for tile in range(6):
            if tile < 4:
                col = first + tile * LANE + lane
            else:
                col = first + (tile - 4) * HALF + edge
            good = (col >= low) & (col <= row)
            msc_ref[tile, lag * EXT : (lag + 1) * EXT, :] = jnp.where(good, scale, 0.0).astype(F32)


def build_bands(cw_ref, base_ref, w_ref):
    base_ref[...] = jnp.zeros_like(base_ref)
    center = (iota((LAGS, REACH), 0) == 0) & (iota((LAGS, REACH), 1) == REACH // 2)
    for h in range(HEADS):
        taps = cw_ref[h].astype(F32) + center.astype(F32)
        base_ref[8 * h : 8 * h + LAGS, 0:REACH] = taps
    base_ref[...] = pltpu.roll(base_ref[...], LANE - SIDE, 1)
    w_ref[...] = jnp.zeros_like(w_ref)
    diff = iota((LANE, LANE), 1) - iota((LANE, LANE), 0)
    near = (diff <= SIDE) & (diff >= -SIDE)
    blank = jnp.zeros((8, LANE), F32)

    def one_head(h, carry):
        base = base_ref[pl.ds(pl.multiple_of(h * 8, 8), 8), :]
        for a in range(LAGS):
            ring = jnp.broadcast_to(base[a : a + 1, :], (LANE, LANE))
            ring = pltpu.roll(ring, 0, 1, stride=1, stride_axis=0)
            diag = jnp.where(near, ring, 0.0).astype(BF16)
            upper = jnp.where(diff[LANE - 8 :] <= SIDE - LANE, ring[LANE - 8 :], 0.0)
            lower = jnp.where(diff[:8] >= LANE - SIDE, ring[:8], 0.0)
            top = a * HALF
            w_ref[h, top : top + LANE, 0:LANE] = diag
            w_ref[h, top + LANE : top + HALF, LANE:HALF] = diag
            w_ref[h, top + LANE - 16 : top + LANE, LANE:HALF] = jnp.concatenate(
                [blank, upper], axis=0
            ).astype(BF16)
            w_ref[h, top + LANE : top + LANE + 16, 0:LANE] = jnp.concatenate(
                [lower, blank], axis=0
            ).astype(BF16)
            edge = LAGS * HALF + 16 * a
            w_ref[h, edge : edge + 16, 0:LANE] = jnp.concatenate([upper, blank], axis=0).astype(BF16)
            w_ref[h, edge : edge + 16, LANE:HALF] = jnp.concatenate(
                [blank, lower], axis=0
            ).astype(BF16)
        return carry

    lax.fori_loop(0, HEADS, one_head, 0)


def build_edges(k_ref, kn_ref, kt_ref):
    left = [kn_ref[0], k_ref[HALF - 16 : HALF, :]]
    right = [k_ref[HALF : HALF + 16, :], kn_ref[1]]
    for t in range(2):
        pair = jnp.concatenate([left[t].astype(F32)[8:16], right[t].astype(F32)[0:8]], axis=0)
        pair = pair.astype(BF16)
        for a in range(8):
            kt_ref[t * LANE + 16 * a : t * LANE + 16 * a + 16, :] = pair


def attend_group(
    g, arrive, mw_ref, qg_ref, qh_ref, k_ref, v_ref, kt_ref, w_ref, msc_ref, scratch, ob_ref, st_ref
):
    msk_ref, x_ref, conv_ref, probs_ref, row_ref = scratch
    lane = iota((CHUNK, LANE), 1)

    def one_head(p, carry):
        h = g * GROUP + p
        cols = pl.ds(pl.multiple_of(h * LANE, LANE), LANE)
        arrive(h)
        for lag in range(SPAN):
            edge = qh_ref[g, lag, :, pl.ds(pl.multiple_of(p * LANE, LANE), LANE)].astype(F32)
            edge = jnp.concatenate([edge, edge], axis=0).astype(BF16)
            qg_ref[h, lag * EXT : lag * EXT + HALO, :] = edge
        q = qg_ref[h]
        for t in range(3):
            keys = k_ref[t * HALF : (t + 1) * HALF, cols] if t < 2 else kt_ref[:, cols]
            logits = dot_nt(q, keys)
            for u in range(2):
                msk_ref[2 * t + u] = logits[:, u * LANE : (u + 1) * LANE] * msc_ref[2 * t + u]
        for lag in range(SPAN):
            base = lag * EXT + HALO
            for t in range(2):
                to = t * ROWS + lag * CHUNK
                for a in range(LAGS):
                    for u in range(2):
                        piece = msk_ref[2 * t + u, base - a : base - a + CHUNK, :]
                        at = a * HALF + u * LANE
                        x_ref[to : to + CHUNK, at : at + LANE] = piece.astype(BF16)
                piece = msk_ref[4 + t, base : base + CHUNK, :]
                for a in range(1, LAGS):
                    other = msk_ref[4 + t, base - a : base - a + CHUNK, :]
                    piece = jnp.where(lane >= 16 * a, other, piece)
                x_ref[to : to + CHUNK, LAGS * HALF : DEPTH] = piece.astype(BF16)
        conv_ref[p] = jnp.dot(x_ref[...], w_ref[h], preferred_element_type=F32)
        return carry

    lax.fori_loop(0, GROUP, one_head, 0)
    weights = [
        [mw_ref[g, p, q] + (1.0 if p == q else 0.0) for q in range(GROUP)] for p in range(GROUP)
    ]
    small = iota((16, LANE), 1)

    def soft_rows(b, carry):
        row = pl.multiple_of(b * 16, 16)
        erow = pl.multiple_of((b + b // 4 + 1) * 16, 16)
        good = [msc_ref[tile, pl.ds(erow, 16), :] > 0 for tile in range(4)]
        conv = [
            [
                conv_ref[q, pl.ds(pl.multiple_of((tile // 2) * ROWS + row, 16), 16),
                         (tile % 2) * LANE : (tile % 2 + 1) * LANE]
                for tile in range(4)
            ]
            for q in range(GROUP)
        ]
        stats = jnp.zeros((16, LANE), F32)
        for p in range(GROUP):
            mixed = []
            for tile in range(4):
                total = conv[0][tile] * weights[p][0]
                for q in range(1, GROUP):
                    total = total + conv[q][tile] * weights[p][q]
                mixed.append(jnp.where(good[tile], total, LOW))
            top = jnp.maximum(jnp.maximum(mixed[0], mixed[1]), jnp.maximum(mixed[2], mixed[3]))
            top = jnp.max(top, axis=1, keepdims=True)
            expo = [jnp.exp(m - top) for m in mixed]
            for tile in range(4):
                probs_ref[p, pl.ds(row, 16), tile * LANE : (tile + 1) * LANE] = expo[tile].astype(BF16)
            total = jnp.sum((expo[0] + expo[1]) + (expo[2] + expo[3]), axis=1, keepdims=True)
            stats = jnp.where(small == p, top, stats)
            stats = jnp.where(small == GROUP + p, total, stats)
        row_ref[pl.ds(row, 16), :] = stats
        return carry

    lax.fori_loop(0, ROWS // 16, soft_rows, 0)
    for pair in range(3):
        st_ref[g, pair] = row_ref[pair * LANE : (pair + 1) * LANE, :].T[0:8, :]

    def one_out(p, carry):
        cols = pl.ds(pl.multiple_of((g * GROUP + p) * LANE, LANE), LANE)
        out = jnp.dot(probs_ref[p], v_ref[:, cols], preferred_element_type=F32)
        ob_ref[:, cols] = out.astype(BF16)
        return carry

    lax.fori_loop(0, GROUP, one_out, 0)


def combine_group(g, og_ref, sg_ref, fin_ref):
    tiles = sg_ref[g].reshape(16 * 8, LANE).T
    parts = []
    for lag in range(SPAN):
        at = (lag % 2) * CHUNK
        part = tiles[at : at + CHUNK, :]
        parts.append(pltpu.roll(part, LANE - 8 * lag, 1) if lag else part)
    top = parts[0]
    for part in parts[1:]:
        top = jnp.maximum(top, part)
    scales = [jnp.exp(part - top) for part in parts]
    total = jnp.zeros((CHUNK, LANE), F32)
    for part, scale in zip(parts, scales):
        total = total + scale * pltpu.roll(part, LANE - GROUP, 1)
    for p in range(GROUP):
        cols = pl.ds(pl.multiple_of((g * GROUP + p) * LANE, LANE), LANE)
        acc = jnp.zeros((CHUNK, LANE), F32)
        for lag in range(SPAN):
            acc = acc + og_ref[lag, :, cols].astype(F32) * scales[lag][:, p : p + 1]
        fin_ref[:, cols] = (acc / total[:, p : p + 1]).astype(BF16)


def kernel(
    q_hbm, k_hbm, v_hbm, cw_ref, mw_ref, doc_ref, out_hbm,
    qg_ref, qh_ref, k_ref, v_ref, kn_ref, kt_ref, base_ref, w_ref, msc_ref,
    msk_ref, x_ref, conv_ref, probs_ref, row_ref, ob_ref, st_ref, og_ref, sg_ref, fin_ref,
    local_sem, q_send, q_recv, h_send, h_recv, n_send, n_recv, o_send, o_recv, s_send, s_recv,
    f_send, f_recv,
):
    qb, kb = lax.axis_index("qb"), lax.axis_index("kb")
    mine = qb * 16 + kb
    after = mine + 1
    join = joined(qb, kb)
    chunks = [served(qb, kb, lag) for lag in range(SPAN)]

    def is_me(where):
        return jnp.logical_and(where[0] == qb, where[1] == kb)

    def both(a, b):
        return jnp.logical_and(a, b)

    def place(where):
        return {"qb": where[0], "kb": where[1]}

    true = kb >= 0
    works = [kb + lag <= 15 for lag in range(SPAN)]
    sends = [mine // 8 >= lag for lag in range(SPAN)]
    halos = [both(after <= 127, after // 8 >= lag) for lag in range(SPAN)]
    joins = [join // 8 >= lag for lag in range(SPAN)]
    halo_in = [both(works[lag], chunks[lag] > 0) for lag in range(SPAN)]

    load_k = pltpu.make_async_copy(k_hbm, k_ref, local_sem.at[0])
    load_v = pltpu.make_async_copy(v_hbm, v_ref, local_sem.at[1])
    load_k.start()
    load_v.start()

    @pl.when(kb == 0)
    def _():
        kn_ref[0] = jnp.zeros((16, WIDTH), BF16)
        for g in range(GROUPS):
            qh_ref[g, 0] = jnp.zeros((8, HALFW), BF16)

    @pl.when(kb == 15)
    def _():
        kn_ref[1] = jnp.zeros((16, WIDTH), BF16)

    for lag in range(SPAN):
        @pl.when(jnp.logical_not(joins[lag]))
        def _():
            og_ref[lag] = jnp.zeros((CHUNK, WIDTH), BF16)
    sg_ref[...] = jnp.full(sg_ref.shape, LOW, F32)

    barrier = pltpu.get_barrier_semaphore()
    peers = [((qb, kb + 1), kb < 15), ((qb, kb - 1), kb > 0)]
    for lag in range(SPAN):
        peers.append((worker(mine, lag), sends[lag]))
        peers.append((worker(after, lag), halos[lag]))
        peers.append((owner(chunks[lag]), works[lag]))
        peers.append((owner(chunks[lag] - 1), halo_in[lag]))
        peers.append((joiner(chunks[lag]), works[lag]))
        peers.append((worker(join, lag), joins[lag]))
    peers.append((owner(join), true))
    peers.append((joiner(mine), true))
    count = jnp.int32(0)
    for where, ok in peers:
        go = both(ok, jnp.logical_not(is_me(where)))

        @pl.when(go)
        def _():
            pl.semaphore_signal(barrier, inc=1, device_id=place(where), device_id_type=MESH)

        count = count + go.astype(jnp.int32)

    build_masks(qb, kb, doc_ref, msc_ref)
    build_bands(cw_ref, base_ref, w_ref)
    pl.semaphore_wait(barrier, count)

    def remote(src, dst, send, recv, where):
        return pltpu.make_async_remote_copy(
            src_ref=src, dst_ref=dst, send_sem=send, recv_sem=recv,
            device_id=place(where), device_id_type=MESH,
        )

    def start(parts, where, ok):
        src, dst, send, recv = parts
        here = is_me(where)

        @pl.when(both(ok, jnp.logical_not(here)))
        def _():
            remote(src, dst, send, recv, where).start()

        @pl.when(both(ok, here))
        def _():
            pltpu.make_async_copy(src, dst, recv).start()

    def sent(parts, where, ok):
        src, dst, send, recv = parts

        @pl.when(both(ok, jnp.logical_not(is_me(where))))
        def _():
            remote(src, dst, send, recv, where).wait_send()

    def landed(parts, where, ok):
        src, dst, send, recv = parts
        here = is_me(where)

        @pl.when(both(ok, jnp.logical_not(here)))
        def _():
            remote(src, dst, send, recv, where).wait_recv()

        @pl.when(both(ok, here))
        def _():
            pltpu.make_async_copy(src, dst, recv).wait()

    def lanes(start, size):
        return pl.ds(pl.multiple_of(start * size, size), size)

    def chunk_parts(h, lag):
        return (
            q_hbm.at[:, lanes(h, LANE)], qg_ref.at[h, lag * EXT + HALO : (lag + 1) * EXT, :],
            q_send.at[h, lag], q_recv.at[h, lag],
        )

    def halo_parts(g, lag):
        return (
            q_hbm.at[CHUNK - 8 : CHUNK, lanes(g, HALFW)], qh_ref.at[g, lag],
            h_send.at[g, lag], h_recv.at[g, lag],
        )

    def out_parts(g, lag):
        cols = lanes(g, HALFW)
        return (
            ob_ref.at[lag * CHUNK : (lag + 1) * CHUNK, cols], og_ref.at[lag, :, cols],
            o_send.at[g, lag], o_recv.at[g, lag],
        )

    def stat_parts(g, lag):
        return st_ref.at[g, lag // 2], sg_ref.at[g, lag], s_send.at[g, lag], s_recv.at[g, lag]

    def final_parts(g):
        cols = lanes(g, HALFW)
        return fin_ref.at[:, cols], out_hbm.at[:, cols], f_send.at[g], f_recv.at[g]

    edges = [
        ((k_hbm.at[BLOCK - 16 : BLOCK, :], kn_ref.at[0], n_send.at[0], n_recv.at[0]),
         (qb, kb + 1), kb < 15, (qb, kb - 1), kb > 0),
        ((k_hbm.at[0:16, :], kn_ref.at[1], n_send.at[1], n_recv.at[1]),
         (qb, kb - 1), kb > 0, (qb, kb + 1), kb < 15),
    ]
    for parts, where, ok, _, _ in edges:
        start(parts, where, ok)

    def send_group(g, carry):
        for lag in range(SPAN):
            start(halo_parts(g, lag), worker(after, lag), halos[lag])

        def send_head(p, carry):
            for lag in range(SPAN):
                start(chunk_parts(g * GROUP + p, lag), worker(mine, lag), sends[lag])
            return carry

        return lax.fori_loop(0, GROUP, send_head, carry)

    lax.fori_loop(0, GROUPS, send_group, 0)

    load_k.wait()
    for parts, _, _, where, ok in edges:
        landed(parts, where, ok)
    build_edges(k_ref, kn_ref, kt_ref)
    load_v.wait()

    def arrive(h):
        for lag in range(SPAN):
            landed(chunk_parts(h, lag), owner(chunks[lag]), works[lag])

    def one_group(g, carry):
        for lag in range(SPAN):
            landed(halo_parts(g, lag), owner(chunks[lag] - 1), halo_in[lag])
        attend_group(
            g, arrive, mw_ref, qg_ref, qh_ref, k_ref, v_ref, kt_ref, w_ref, msc_ref,
            (msk_ref, x_ref, conv_ref, probs_ref, row_ref), ob_ref, st_ref,
        )
        for lag in range(SPAN):
            start(stat_parts(g, lag), joiner(chunks[lag]), works[lag])
            start(out_parts(g, lag), joiner(chunks[lag]), works[lag])
        return carry

    lax.fori_loop(0, GROUPS, one_group, 0)

    def one_result(g, carry):
        for lag in range(SPAN):
            landed(stat_parts(g, lag), worker(join, lag), joins[lag])
            landed(out_parts(g, lag), worker(join, lag), joins[lag])
        combine_group(g, og_ref, sg_ref, fin_ref)
        start(final_parts(g), owner(join), true)
        return carry

    lax.fori_loop(0, GROUPS, one_result, 0)

    for parts, where, ok, _, _ in edges:
        sent(parts, where, ok)

    def drain(g, carry):
        landed(final_parts(g), joiner(mine), true)
        sent(final_parts(g), owner(join), true)
        for lag in range(SPAN):
            sent(halo_parts(g, lag), worker(after, lag), halos[lag])
            sent(stat_parts(g, lag), joiner(chunks[lag]), works[lag])
            sent(out_parts(g, lag), joiner(chunks[lag]), works[lag])

        def drain_head(p, carry):
            for lag in range(SPAN):
                sent(chunk_parts(g * GROUP + p, lag), worker(mine, lag), sends[lag])
            return carry

        return lax.fori_loop(0, GROUP, drain_head, carry)

    lax.fori_loop(0, GROUPS, drain, 0)


def body(queries, keys, values, conv_weight, mix_weight, doc_ids):
    docs = doc_ids.reshape(-1, LANE)
    any_space = pl.BlockSpec(memory_space=pl.ANY)
    vmem = pl.BlockSpec(memory_space=pltpu.VMEM)
    dma = pltpu.SemaphoreType.DMA
    return pl.pallas_call(
        kernel,
        out_shape=jax.ShapeDtypeStruct((CHUNK, WIDTH), BF16),
        in_specs=[
            any_space, any_space, any_space, vmem, pl.BlockSpec(memory_space=pltpu.SMEM), vmem,
        ],
        out_specs=any_space,
        scratch_shapes=[
            pltpu.VMEM((HEADS, EROWS, LANE), BF16),
            pltpu.VMEM((GROUPS, SPAN, 8, HALFW), BF16),
            pltpu.VMEM((BLOCK, WIDTH), BF16),
            pltpu.VMEM((BLOCK, WIDTH), BF16),
            pltpu.VMEM((2, 16, WIDTH), BF16),
            pltpu.VMEM((2 * LANE, WIDTH), BF16),
            pltpu.VMEM((8 * HEADS, LANE), F32),
            pltpu.VMEM((HEADS, DEPTH, HALF), BF16),
            pltpu.VMEM((6, EROWS, LANE), F32),
            pltpu.VMEM((6, EROWS, LANE), F32),
            pltpu.VMEM((2 * ROWS, DEPTH), BF16),
            pltpu.VMEM((GROUP, 2 * ROWS, HALF), F32),
            pltpu.VMEM((GROUP, ROWS, BLOCK), BF16),
            pltpu.VMEM((3 * LANE, LANE), F32),
            pltpu.VMEM((ROWS, WIDTH), BF16),
            pltpu.VMEM((GROUPS, 3, 8, LANE), F32),
            pltpu.VMEM((SPAN, CHUNK, WIDTH), BF16),
            pltpu.VMEM((GROUPS, 16, 8, LANE), F32),
            pltpu.VMEM((CHUNK, WIDTH), BF16),
            dma((2,)),
            dma((HEADS, SPAN)), dma((HEADS, SPAN)),
            dma((GROUPS, SPAN)), dma((GROUPS, SPAN)),
            dma((2,)), dma((2,)),
            dma((GROUPS, SPAN)), dma((GROUPS, SPAN)),
            dma((GROUPS, SPAN)), dma((GROUPS, SPAN)),
            dma((GROUPS,)), dma((GROUPS,)),
        ],
        compiler_params=pltpu.CompilerParams(collective_id=0, has_side_effects=True),
    )(queries, keys, values, conv_weight, mix_weight, docs)


def solution(mesh):
    placed = (
        P(("ba", "qb", "kb"), None),
        P(("ba", "kb"), None),
        P(("ba", "kb"), None),
        P(),
        P(),
        P("ba"),
    )
    return jax.shard_map(
        body, mesh=mesh, in_specs=placed, out_specs=P(("ba", "qb", "kb"), None), check_vma=False
    )
```

```python
import math

import jax
import jax.numpy as jnp
from jax import lax
from jax.experimental import pallas as pl
from jax.experimental.pallas import tpu as pltpu
from jax.sharding import PartitionSpec as P

MESH = pl.DeviceIdType.MESH
F32 = jnp.float32
BF16 = jnp.bfloat16

CHUNK = 64
HALO = 16
EXT = CHUNK + HALO
TURN = (2, 4)
SPAN = 5
BLOCK = 512
HALF = 256
LANE = 128
LAGS = 6
REACH = 11
SIDE = 5
HEADS = 8
GROUP = 4
GROUPS = 2
DEPTH = LAGS * HALF + LANE
ROWS = SPAN * CHUNK
EROWS = SPAN * EXT
HALFW = GROUP * LANE
LOW = -1e30
WIDTH = HEADS * LANE


def shift(group):
    return 5 * (group // 2) + TURN[0] + (TURN[1] - TURN[0]) * (group % 2)


def column(chunk):
    return (chunk % 8 + 64 - shift(chunk // 8)) % 8


def worker(chunk, lag):
    return column(chunk), chunk // 8 - lag


def relay(chunk):
    return column(chunk), chunk % 16


def owner(chunk):
    return chunk // 16, chunk % 16


def served(qb, kb, lag):
    group = kb + lag
    return group * 8 + (qb + shift(group)) % 8


def relayed(qb, kb):
    turn = TURN[0] + (TURN[1] - TURN[0]) * (kb // 8)
    return (5 * (kb % 8 + 16 - turn - qb)) % 8 * 16 + kb


def iota(shape, dim):
    return lax.broadcasted_iota(jnp.int32, shape, dim)


def dot_nt(a, b):
    return lax.dot_general(a, b, (((1,), (1,)), ((), ())), preferred_element_type=F32)


def build_masks(qb, kb, doc_ref, msc_ref):
    scale = 1.0 / math.sqrt(LANE)
    docs = doc_ref[...]
    starts = []
    for value in range(1, 8):
        below = (docs < value).astype(F32)
        below = jnp.sum(jnp.sum(below, axis=0, keepdims=True), axis=1, keepdims=True)
        starts.append(jnp.broadcast_to(below.astype(jnp.int32), (EXT, LANE)))
    lane = iota((EXT, LANE), 1)
    first = kb * BLOCK
    edge = lane % 16
    edge = jnp.where(edge < 8, edge - 8, edge + (HALF - 8))
    for lag in range(SPAN):
        row = served(qb, kb, lag) * CHUNK - HALO + iota((EXT, LANE), 0)
        low = jnp.zeros((EXT, LANE), jnp.int32)
        for start in starts:
            low = jnp.where(start <= row, start, low)
        for tile in range(6):
            if tile < 4:
                col = first + tile * LANE + lane
            else:
                col = first + (tile - 4) * HALF + edge
            good = (col >= low) & (col <= row)
            msc_ref[tile, lag * EXT : (lag + 1) * EXT, :] = jnp.where(good, scale, 0.0).astype(F32)


def build_bands(cw_ref, base_ref, w_ref):
    base_ref[...] = jnp.zeros_like(base_ref)
    center = (iota((HEADS, REACH), 1) == REACH // 2).astype(F32)
    for a in range(LAGS):
        taps = cw_ref[a].astype(F32)
        base_ref[8 * a : 8 * a + HEADS, 0:REACH] = taps + center if a == 0 else taps
    base_ref[...] = pltpu.roll(base_ref[...], LANE - SIDE, 1)
    w_ref[...] = jnp.zeros_like(w_ref)
    diff = iota((LANE, LANE), 1) - iota((LANE, LANE), 0)
    near = (diff <= SIDE) & (diff >= -SIDE)
    blank = jnp.zeros((8, LANE), F32)

    def one_head(h, carry):
        for a in range(LAGS):
            ring = jnp.broadcast_to(base_ref[pl.ds(8 * a + h, 1), :], (LANE, LANE))
            ring = pltpu.roll(ring, 0, 1, stride=1, stride_axis=0)
            diag = jnp.where(near, ring, 0.0).astype(BF16)
            upper = jnp.where(diff[LANE - 8 :] <= SIDE - LANE, ring[LANE - 8 :], 0.0)
            lower = jnp.where(diff[:8] >= LANE - SIDE, ring[:8], 0.0)
            top = a * HALF
            w_ref[h, top : top + LANE, 0:LANE] = diag
            w_ref[h, top + LANE : top + HALF, LANE:HALF] = diag
            w_ref[h, top + LANE - 16 : top + LANE, LANE:HALF] = jnp.concatenate(
                [blank, upper], axis=0
            ).astype(BF16)
            w_ref[h, top + LANE : top + LANE + 16, 0:LANE] = jnp.concatenate(
                [lower, blank], axis=0
            ).astype(BF16)
            edge = LAGS * HALF + 16 * a
            w_ref[h, edge : edge + 16, 0:LANE] = jnp.concatenate([upper, blank], axis=0).astype(BF16)
            w_ref[h, edge : edge + 16, LANE:HALF] = jnp.concatenate(
                [blank, lower], axis=0
            ).astype(BF16)
        return carry

    lax.fori_loop(0, HEADS, one_head, 0)


def build_edges(k_ref, kn_ref, kt_ref):
    left = [kn_ref[0], k_ref[HALF - 16 : HALF, :]]
    right = [k_ref[HALF : HALF + 16, :], kn_ref[1]]
    for t in range(2):
        pair = jnp.concatenate([left[t].astype(F32)[8:16], right[t].astype(F32)[0:8]], axis=0)
        pair = pair.astype(BF16)
        for a in range(8):
            kt_ref[t * LANE + 16 * a : t * LANE + 16 * a + 16, :] = pair


def attend_group(
    g, arrive, mw_ref, qg_ref, qh_ref, k_ref, v_ref, kt_ref, w_ref, msc_ref, scratch, ob_ref, st_ref
):
    msk_ref, x_ref, conv_ref, probs_ref, row_ref = scratch
    lane = iota((CHUNK, LANE), 1)

    def one_head(p, carry):
        h = g * GROUP + p
        cols = pl.ds(pl.multiple_of(h * LANE, LANE), LANE)
        arrive(h)
        for lag in range(SPAN):
            edge = qh_ref[g, lag, :, pl.ds(pl.multiple_of(p * LANE, LANE), LANE)].astype(F32)
            edge = jnp.concatenate([edge, edge], axis=0).astype(BF16)
            qg_ref[h, lag * EXT : lag * EXT + HALO, :] = edge
        q = qg_ref[h]
        for t in range(3):
            keys = k_ref[t * HALF : (t + 1) * HALF, cols] if t < 2 else kt_ref[:, cols]
            logits = dot_nt(q, keys)
            for u in range(2):
                msk_ref[2 * t + u] = logits[:, u * LANE : (u + 1) * LANE] * msc_ref[2 * t + u]
        for lag in range(SPAN):
            base = lag * EXT + HALO
            for t in range(2):
                to = t * ROWS + lag * CHUNK
                for a in range(LAGS):
                    for u in range(2):
                        piece = msk_ref[2 * t + u, base - a : base - a + CHUNK, :]
                        at = a * HALF + u * LANE
                        x_ref[to : to + CHUNK, at : at + LANE] = piece.astype(BF16)
                piece = msk_ref[4 + t, base : base + CHUNK, :]
                for a in range(1, LAGS):
                    other = msk_ref[4 + t, base - a : base - a + CHUNK, :]
                    piece = jnp.where(lane >= 16 * a, other, piece)
                x_ref[to : to + CHUNK, LAGS * HALF : DEPTH] = piece.astype(BF16)
        conv_ref[p] = jnp.dot(x_ref[...], w_ref[h], preferred_element_type=F32)
        return carry

    lax.fori_loop(0, GROUP, one_head, 0)
    weights = [
        [mw_ref[g, p, q] + (1.0 if p == q else 0.0) for q in range(GROUP)] for p in range(GROUP)
    ]
    small = iota((16, LANE), 1)

    def soft_rows(b, carry):
        row = pl.multiple_of(b * 16, 16)
        erow = pl.multiple_of((b + b // 4 + 1) * 16, 16)
        good = [msc_ref[tile, pl.ds(erow, 16), :] > 0 for tile in range(4)]
        conv = [
            [
                conv_ref[q, pl.ds(pl.multiple_of((tile // 2) * ROWS + row, 16), 16),
                         (tile % 2) * LANE : (tile % 2 + 1) * LANE]
                for tile in range(4)
            ]
            for q in range(GROUP)
        ]
        stats = jnp.zeros((16, LANE), F32)
        for p in range(GROUP):
            mixed = []
            for tile in range(4):
                total = conv[0][tile] * weights[p][0]
                for q in range(1, GROUP):
                    total = total + conv[q][tile] * weights[p][q]
                mixed.append(jnp.where(good[tile], total, LOW))
            top = jnp.maximum(jnp.maximum(mixed[0], mixed[1]), jnp.maximum(mixed[2], mixed[3]))
            top = jnp.max(top, axis=1, keepdims=True)
            expo = [jnp.exp(m - top) for m in mixed]
            for tile in range(4):
                probs_ref[p, pl.ds(row, 16), tile * LANE : (tile + 1) * LANE] = expo[tile].astype(BF16)
            total = jnp.sum((expo[0] + expo[1]) + (expo[2] + expo[3]), axis=1, keepdims=True)
            stats = jnp.where(small == p, top, stats)
            stats = jnp.where(small == GROUP + p, total, stats)
        row_ref[pl.ds(row, 16), :] = stats
        return carry

    lax.fori_loop(0, ROWS // 16, soft_rows, 0)
    for pair in range(3):
        st_ref[g, pair] = row_ref[pair * LANE : (pair + 1) * LANE, :].T[0:8, :]

    def one_out(p, carry):
        cols = pl.ds(pl.multiple_of((g * GROUP + p) * LANE, LANE), LANE)
        out = jnp.dot(probs_ref[p], v_ref[:, cols], preferred_element_type=F32)
        ob_ref[:, cols] = out.astype(BF16)
        return carry

    lax.fori_loop(0, GROUP, one_out, 0)


def combine_group(g, og_ref, sg_ref, out_ref):
    tiles = sg_ref[g].reshape(16 * 8, LANE).T
    parts = []
    for lag in range(SPAN):
        at = (lag % 2) * CHUNK
        part = tiles[at : at + CHUNK, :]
        parts.append(pltpu.roll(part, LANE - 8 * lag, 1) if lag else part)
    top = parts[0]
    for part in parts[1:]:
        top = jnp.maximum(top, part)
    scales = [jnp.exp(part - top) for part in parts]
    total = jnp.zeros((CHUNK, LANE), F32)
    for part, scale in zip(parts, scales):
        total = total + scale * pltpu.roll(part, LANE - GROUP, 1)
    for p in range(GROUP):
        cols = pl.ds(pl.multiple_of((g * GROUP + p) * LANE, LANE), LANE)
        acc = jnp.zeros((CHUNK, LANE), F32)
        for lag in range(SPAN):
            acc = acc + og_ref[lag, :, cols].astype(F32) * scales[lag][:, p : p + 1]
        out_ref[:, cols] = (acc / total[:, p : p + 1]).astype(BF16)


def kernel(
    q_hbm, k_hbm, v_hbm, cw_ref, mw_ref, doc_ref, out_ref,
    qg_ref, qh_ref, k_ref, v_ref, kn_ref, kt_ref, base_ref, w_ref, msc_ref,
    msk_ref, x_ref, conv_ref, probs_ref, row_ref, ob_ref, st_ref, og_ref, sg_ref, qr_ref, hr_ref,
    local_sem, q_send, q_recv, h_send, h_recv, n_send, n_recv, o_send, o_recv, s_send, s_recv,
    u_send, u_recv, v_send, v_recv,
):
    qb, kb = lax.axis_index("qb"), lax.axis_index("kb")
    mine = qb * 16 + kb
    after = mine + 1
    held = relayed(qb, kb)
    chunks = [served(qb, kb, lag) for lag in range(SPAN)]

    def is_me(where):
        return jnp.logical_and(where[0] == qb, where[1] == kb)

    def both(a, b):
        return jnp.logical_and(a, b)

    def place(where):
        return {"qb": where[0], "kb": where[1]}

    true = kb >= 0
    works = [kb + lag <= 15 for lag in range(SPAN)]
    sends = [mine // 8 >= lag for lag in range(SPAN)]
    hands = [held // 8 >= lag for lag in range(SPAN)]
    last = mine == 127
    first = held == 0
    halo_out, halo_in = jnp.logical_not(last), jnp.logical_not(first)

    load_k = pltpu.make_async_copy(k_hbm, k_ref, local_sem.at[0])
    load_v = pltpu.make_async_copy(v_hbm, v_ref, local_sem.at[1])
    load_k.start()
    load_v.start()

    @pl.when(kb == 0)
    def _():
        kn_ref[0] = jnp.zeros((16, WIDTH), BF16)

    @pl.when(kb == 15)
    def _():
        kn_ref[1] = jnp.zeros((16, WIDTH), BF16)

    @pl.when(first)
    def _():
        hr_ref[...] = jnp.zeros_like(hr_ref)

    for lag in range(1, SPAN):
        @pl.when(jnp.logical_not(sends[lag]))
        def _():
            og_ref[lag] = jnp.zeros((CHUNK, WIDTH), BF16)
    sg_ref[...] = jnp.full(sg_ref.shape, LOW, F32)

    barrier = pltpu.get_barrier_semaphore()
    peers = [
        ((qb, kb + 1), kb < 15), ((qb, kb - 1), kb > 0),
        (relay(mine), true), (owner(held), true),
        (relay(after), halo_out), (owner(held - 1), halo_in),
    ]
    for lag in range(SPAN):
        peers.append((worker(held, lag), hands[lag]))
        peers.append((relay(chunks[lag]), works[lag]))
        peers.append((owner(chunks[lag]), works[lag]))
        peers.append((worker(mine, lag), sends[lag]))
    count = jnp.int32(0)
    for where, ok in peers:
        go = both(ok, jnp.logical_not(is_me(where)))

        @pl.when(go)
        def _():
            pl.semaphore_signal(barrier, inc=1, device_id=place(where), device_id_type=MESH)

        count = count + go.astype(jnp.int32)

    build_masks(qb, kb, doc_ref, msc_ref)
    build_bands(cw_ref, base_ref, w_ref)
    pl.semaphore_wait(barrier, count)

    def remote(src, dst, send, recv, where):
        return pltpu.make_async_remote_copy(
            src_ref=src, dst_ref=dst, send_sem=send, recv_sem=recv,
            device_id=place(where), device_id_type=MESH,
        )

    def start(parts, where, ok):
        src, dst, send, recv = parts
        here = is_me(where)

        @pl.when(both(ok, jnp.logical_not(here)))
        def _():
            remote(src, dst, send, recv, where).start()

        @pl.when(both(ok, here))
        def _():
            pltpu.make_async_copy(src, dst, recv).start()

    def sent(parts, where, ok):
        src, dst, send, recv = parts

        @pl.when(both(ok, jnp.logical_not(is_me(where))))
        def _():
            remote(src, dst, send, recv, where).wait_send()

    def landed(parts, where, ok):
        src, dst, send, recv = parts
        here = is_me(where)

        @pl.when(both(ok, jnp.logical_not(here)))
        def _():
            remote(src, dst, send, recv, where).wait_recv()

        @pl.when(both(ok, here))
        def _():
            pltpu.make_async_copy(src, dst, recv).wait()

    def lanes(start, size):
        return pl.ds(pl.multiple_of(start * size, size), size)

    def up_parts(h):
        return q_hbm.at[:, lanes(h, LANE)], qr_ref.at[h], u_send.at[h], u_recv.at[h]

    def up_halo_parts(g):
        return (
            q_hbm.at[CHUNK - 8 : CHUNK, lanes(g, HALFW)], hr_ref.at[g], v_send.at[g], v_recv.at[g]
        )

    def chunk_parts(h, lag):
        return (
            qr_ref.at[h], qg_ref.at[h, lag * EXT + HALO : (lag + 1) * EXT, :],
            q_send.at[h, lag], q_recv.at[h, lag],
        )

    def halo_parts(g, lag):
        return hr_ref.at[g], qh_ref.at[g, lag], h_send.at[g, lag], h_recv.at[g, lag]

    def out_parts(g, lag):
        cols = lanes(g, HALFW)
        return (
            ob_ref.at[lag * CHUNK : (lag + 1) * CHUNK, cols], og_ref.at[lag, :, cols],
            o_send.at[g, lag], o_recv.at[g, lag],
        )

    def stat_parts(g, lag):
        return st_ref.at[g, lag // 2], sg_ref.at[g, lag], s_send.at[g, lag], s_recv.at[g, lag]

    edges = [
        ((k_hbm.at[BLOCK - 16 : BLOCK, :], kn_ref.at[0], n_send.at[0], n_recv.at[0]),
         (qb, kb + 1), kb < 15, (qb, kb - 1), kb > 0),
        ((k_hbm.at[0:16, :], kn_ref.at[1], n_send.at[1], n_recv.at[1]),
         (qb, kb - 1), kb > 0, (qb, kb + 1), kb < 15),
    ]
    for parts, where, ok, _, _ in edges:
        start(parts, where, ok)

    def up_group(g, carry):
        start(up_halo_parts(g), relay(after), halo_out)

        def up_head(p, carry):
            start(up_parts(g * GROUP + p), relay(mine), true)
            return carry

        return lax.fori_loop(0, GROUP, up_head, carry)

    lax.fori_loop(0, GROUPS, up_group, 0)

    load_k.wait()
    for parts, _, _, where, ok in edges:
        landed(parts, where, ok)
    build_edges(k_ref, kn_ref, kt_ref)
    load_v.wait()

    def hand_group(g, carry):
        landed(up_halo_parts(g), owner(held - 1), halo_in)
        for lag in range(SPAN):
            start(halo_parts(g, lag), worker(held, lag), hands[lag])

        def hand_head(p, carry):
            h = g * GROUP + p
            landed(up_parts(h), owner(held), true)
            for lag in range(SPAN):
                start(chunk_parts(h, lag), worker(held, lag), hands[lag])
            return carry

        return lax.fori_loop(0, GROUP, hand_head, carry)

    lax.fori_loop(0, GROUPS, hand_group, 0)

    def arrive(h):
        for lag in range(SPAN):
            landed(chunk_parts(h, lag), relay(chunks[lag]), works[lag])

    def one_group(g, carry):
        for lag in range(SPAN):
            landed(halo_parts(g, lag), relay(chunks[lag]), works[lag])
        attend_group(
            g, arrive, mw_ref, qg_ref, qh_ref, k_ref, v_ref, kt_ref, w_ref, msc_ref,
            (msk_ref, x_ref, conv_ref, probs_ref, row_ref), ob_ref, st_ref,
        )
        for lag in range(SPAN):
            start(stat_parts(g, lag), owner(chunks[lag]), works[lag])
            start(out_parts(g, lag), owner(chunks[lag]), works[lag])
        return carry

    lax.fori_loop(0, GROUPS, one_group, 0)

    def one_result(g, carry):
        for lag in range(SPAN):
            landed(stat_parts(g, lag), worker(mine, lag), sends[lag])
            landed(out_parts(g, lag), worker(mine, lag), sends[lag])
        combine_group(g, og_ref, sg_ref, out_ref)
        return carry

    lax.fori_loop(0, GROUPS, one_result, 0)

    for parts, where, ok, _, _ in edges:
        sent(parts, where, ok)

    def drain(g, carry):
        sent(up_halo_parts(g), relay(after), halo_out)
        for lag in range(SPAN):
            sent(halo_parts(g, lag), worker(held, lag), hands[lag])
            sent(stat_parts(g, lag), owner(chunks[lag]), works[lag])
            sent(out_parts(g, lag), owner(chunks[lag]), works[lag])

        def drain_head(p, carry):
            h = g * GROUP + p
            sent(up_parts(h), relay(mine), true)
            for lag in range(SPAN):
                sent(chunk_parts(h, lag), worker(held, lag), hands[lag])
            return carry

        return lax.fori_loop(0, GROUP, drain_head, carry)

    lax.fori_loop(0, GROUPS, drain, 0)


def body(queries, keys, values, conv_weight, mix_weight, doc_ids):
    docs = doc_ids.reshape(-1, LANE)
    taps = conv_weight.transpose(1, 0, 2)
    any_space = pl.BlockSpec(memory_space=pl.ANY)
    vmem = pl.BlockSpec(memory_space=pltpu.VMEM)
    dma = pltpu.SemaphoreType.DMA
    return pl.pallas_call(
        kernel,
        out_shape=jax.ShapeDtypeStruct((CHUNK, WIDTH), BF16),
        in_specs=[
            any_space, any_space, any_space, vmem, pl.BlockSpec(memory_space=pltpu.SMEM), vmem,
        ],
        out_specs=vmem,
        scratch_shapes=[
            pltpu.VMEM((HEADS, EROWS, LANE), BF16),
            pltpu.VMEM((GROUPS, SPAN, 8, HALFW), BF16),
            pltpu.VMEM((BLOCK, WIDTH), BF16),
            pltpu.VMEM((BLOCK, WIDTH), BF16),
            pltpu.VMEM((2, 16, WIDTH), BF16),
            pltpu.VMEM((2 * LANE, WIDTH), BF16),
            pltpu.VMEM((8 * LAGS, LANE), F32),
            pltpu.VMEM((HEADS, DEPTH, HALF), BF16),
            pltpu.VMEM((6, EROWS, LANE), F32),
            pltpu.VMEM((6, EROWS, LANE), F32),
            pltpu.VMEM((2 * ROWS, DEPTH), BF16),
            pltpu.VMEM((GROUP, 2 * ROWS, HALF), F32),
            pltpu.VMEM((GROUP, ROWS, BLOCK), BF16),
            pltpu.VMEM((3 * LANE, LANE), F32),
            pltpu.VMEM((ROWS, WIDTH), BF16),
            pltpu.VMEM((GROUPS, 3, 8, LANE), F32),
            pltpu.VMEM((SPAN, CHUNK, WIDTH), BF16),
            pltpu.VMEM((GROUPS, 16, 8, LANE), F32),
            pltpu.VMEM((HEADS, CHUNK, LANE), BF16),
            pltpu.VMEM((GROUPS, 8, HALFW), BF16),
            dma((2,)),
            dma((HEADS, SPAN)), dma((HEADS, SPAN)),
            dma((GROUPS, SPAN)), dma((GROUPS, SPAN)),
            dma((2,)), dma((2,)),
            dma((GROUPS, SPAN)), dma((GROUPS, SPAN)),
            dma((GROUPS, SPAN)), dma((GROUPS, SPAN)),
            dma((HEADS,)), dma((HEADS,)),
            dma((GROUPS,)), dma((GROUPS,)),
        ],
        compiler_params=pltpu.CompilerParams(collective_id=0, has_side_effects=True),
    )(queries, keys, values, taps, mix_weight, docs)


def solution(mesh):
    placed = (
        P(("ba", "qb", "kb"), None),
        P(("ba", "kb"), None),
        P(("ba", "kb"), None),
        P(),
        P(),
        P("ba"),
    )
    return jax.shard_map(
        body, mesh=mesh, in_specs=placed, out_specs=P(("ba", "qb", "kb"), None), check_vma=False
    )
```

```python
import math

import jax
import jax.numpy as jnp
from jax import lax
from jax.experimental import pallas as pl
from jax.experimental.pallas import tpu as pltpu
from jax.sharding import PartitionSpec as P

MESH = pl.DeviceIdType.MESH
F32 = jnp.float32
BF16 = jnp.bfloat16

CHUNK = 64
HALO = 16
EXT = CHUNK + HALO
SPAN = 5
BLOCK = 512
HALF = 256
LANE = 128
LAGS = 6
REACH = 11
SIDE = 5
HEADS = 8
GROUP = 4
GROUPS = 2
DEPTH = LAGS * HALF + LANE
ROWS = SPAN * CHUNK
EROWS = SPAN * EXT
HALFW = GROUP * LANE
LOW = -1e30
WIDTH = HEADS * LANE


def swap(code):
    return code % 2 * 2 + code // 2


def shift(group):
    return swap((group + 2) % 4) + 3 * plane(group)


def plane(group):
    return (group + 14) % 16 // 4


def column(chunk):
    return (chunk % 8 + 64 - shift(chunk // 8)) % 8


def worker(chunk, lag):
    return column(chunk), chunk // 8 - lag


def relay(chunk):
    return column(chunk), plane(chunk // 8) * 4 + chunk % 4


def owner(chunk):
    return chunk // 16, chunk % 16


def served(qb, kb, lag):
    group = kb + lag
    return group * 8 + (qb + shift(group)) % 8


def relayed(qb, kb):
    level = kb // 4
    code = (kb + 64 - qb - 3 * level) % 4
    group = (4 * level + 2 + swap(code)) % 16
    return group * 8 + (qb + code + 3 * level) % 8


def iota(shape, dim):
    return lax.broadcasted_iota(jnp.int32, shape, dim)


def dot_nt(a, b):
    return lax.dot_general(a, b, (((1,), (1,)), ((), ())), preferred_element_type=F32)


def build_masks(qb, kb, doc_ref, msc_ref):
    scale = 1.0 / math.sqrt(LANE)
    docs = doc_ref[...]
    starts = []
    for value in range(1, 8):
        below = (docs < value).astype(F32)
        below = jnp.sum(jnp.sum(below, axis=0, keepdims=True), axis=1, keepdims=True)
        starts.append(jnp.broadcast_to(below.astype(jnp.int32), (EXT, LANE)))
    lane = iota((EXT, LANE), 1)
    first = kb * BLOCK
    edge = lane % 16
    edge = jnp.where(edge < 8, edge - 8, edge + (HALF - 8))
    for lag in range(SPAN):
        row = served(qb, kb, lag) * CHUNK - HALO + iota((EXT, LANE), 0)
        low = jnp.zeros((EXT, LANE), jnp.int32)
        for start in starts:
            low = jnp.where(start <= row, start, low)
        for tile in range(6):
            if tile < 4:
                col = first + tile * LANE + lane
            else:
                col = first + (tile - 4) * HALF + edge
            good = (col >= low) & (col <= row)
            msc_ref[tile, lag * EXT : (lag + 1) * EXT, :] = jnp.where(good, scale, 0.0).astype(F32)


def build_bands(cw_ref, base_ref, w_ref):
    base_ref[...] = jnp.zeros_like(base_ref)
    center = (iota((HEADS, REACH), 1) == REACH // 2).astype(F32)
    for a in range(LAGS):
        taps = cw_ref[a].astype(F32)
        base_ref[8 * a : 8 * a + HEADS, 0:REACH] = taps + center if a == 0 else taps
    base_ref[...] = pltpu.roll(base_ref[...], LANE - SIDE, 1)
    w_ref[...] = jnp.zeros_like(w_ref)
    diff = iota((LANE, LANE), 1) - iota((LANE, LANE), 0)
    near = (diff <= SIDE) & (diff >= -SIDE)
    blank = jnp.zeros((8, LANE), F32)

    def one_head(h, carry):
        for a in range(LAGS):
            ring = jnp.broadcast_to(base_ref[pl.ds(8 * a + h, 1), :], (LANE, LANE))
            ring = pltpu.roll(ring, 0, 1, stride=1, stride_axis=0)
            diag = jnp.where(near, ring, 0.0).astype(BF16)
            upper = jnp.where(diff[LANE - 8 :] <= SIDE - LANE, ring[LANE - 8 :], 0.0)
            lower = jnp.where(diff[:8] >= LANE - SIDE, ring[:8], 0.0)
            top = a * HALF
            w_ref[h, top : top + LANE, 0:LANE] = diag
            w_ref[h, top + LANE : top + HALF, LANE:HALF] = diag
            w_ref[h, top + LANE - 16 : top + LANE, LANE:HALF] = jnp.concatenate(
                [blank, upper], axis=0
            ).astype(BF16)
            w_ref[h, top + LANE : top + LANE + 16, 0:LANE] = jnp.concatenate(
                [lower, blank], axis=0
            ).astype(BF16)
            edge = LAGS * HALF + 16 * a
            w_ref[h, edge : edge + 16, 0:LANE] = jnp.concatenate([upper, blank], axis=0).astype(BF16)
            w_ref[h, edge : edge + 16, LANE:HALF] = jnp.concatenate(
                [blank, lower], axis=0
            ).astype(BF16)
        return carry

    lax.fori_loop(0, HEADS, one_head, 0)


def build_edges(k_ref, kn_ref, kt_ref):
    left = [kn_ref[0], k_ref[HALF - 16 : HALF, :]]
    right = [k_ref[HALF : HALF + 16, :], kn_ref[1]]
    for t in range(2):
        pair = jnp.concatenate([left[t].astype(F32)[8:16], right[t].astype(F32)[0:8]], axis=0)
        pair = pair.astype(BF16)
        for a in range(8):
            kt_ref[t * LANE + 16 * a : t * LANE + 16 * a + 16, :] = pair


def attend_group(
    g, arrive, mw_ref, qg_ref, qh_ref, k_ref, v_ref, kt_ref, w_ref, msc_ref, scratch, ob_ref, st_ref
):
    msk_ref, x_ref, conv_ref, probs_ref, row_ref = scratch
    lane = iota((CHUNK, LANE), 1)

    def one_head(p, carry):
        h = g * GROUP + p
        cols = pl.ds(pl.multiple_of(h * LANE, LANE), LANE)
        arrive(h)
        for lag in range(SPAN):
            edge = qh_ref[g, lag, :, pl.ds(pl.multiple_of(p * LANE, LANE), LANE)].astype(F32)
            edge = jnp.concatenate([edge, edge], axis=0).astype(BF16)
            qg_ref[h, lag * EXT : lag * EXT + HALO, :] = edge
        q = qg_ref[h]
        for t in range(3):
            keys = k_ref[t * HALF : (t + 1) * HALF, cols] if t < 2 else kt_ref[:, cols]
            logits = dot_nt(q, keys)
            for u in range(2):
                msk_ref[2 * t + u] = logits[:, u * LANE : (u + 1) * LANE] * msc_ref[2 * t + u]
        for lag in range(SPAN):
            base = lag * EXT + HALO
            for t in range(2):
                to = t * ROWS + lag * CHUNK
                for a in range(LAGS):
                    for u in range(2):
                        piece = msk_ref[2 * t + u, base - a : base - a + CHUNK, :]
                        at = a * HALF + u * LANE
                        x_ref[to : to + CHUNK, at : at + LANE] = piece.astype(BF16)
                piece = msk_ref[4 + t, base : base + CHUNK, :]
                for a in range(1, LAGS):
                    other = msk_ref[4 + t, base - a : base - a + CHUNK, :]
                    piece = jnp.where(lane >= 16 * a, other, piece)
                x_ref[to : to + CHUNK, LAGS * HALF : DEPTH] = piece.astype(BF16)
        conv_ref[p] = jnp.dot(x_ref[...], w_ref[h], preferred_element_type=F32)
        return carry

    lax.fori_loop(0, GROUP, one_head, 0)
    weights = [
        [mw_ref[g, p, q] + (1.0 if p == q else 0.0) for q in range(GROUP)] for p in range(GROUP)
    ]
    small = iota((16, LANE), 1)

    def soft_rows(b, carry):
        row = pl.multiple_of(b * 16, 16)
        erow = pl.multiple_of((b + b // 4 + 1) * 16, 16)
        good = [msc_ref[tile, pl.ds(erow, 16), :] > 0 for tile in range(4)]
        conv = [
            [
                conv_ref[q, pl.ds(pl.multiple_of((tile // 2) * ROWS + row, 16), 16),
                         (tile % 2) * LANE : (tile % 2 + 1) * LANE]
                for tile in range(4)
            ]
            for q in range(GROUP)
        ]
        stats = jnp.zeros((16, LANE), F32)
        for p in range(GROUP):
            mixed = []
            for tile in range(4):
                total = conv[0][tile] * weights[p][0]
                for q in range(1, GROUP):
                    total = total + conv[q][tile] * weights[p][q]
                mixed.append(jnp.where(good[tile], total, LOW))
            top = jnp.maximum(jnp.maximum(mixed[0], mixed[1]), jnp.maximum(mixed[2], mixed[3]))
            top = jnp.max(top, axis=1, keepdims=True)
            expo = [jnp.exp(m - top) for m in mixed]
            for tile in range(4):
                probs_ref[p, pl.ds(row, 16), tile * LANE : (tile + 1) * LANE] = expo[tile].astype(BF16)
            total = jnp.sum((expo[0] + expo[1]) + (expo[2] + expo[3]), axis=1, keepdims=True)
            stats = jnp.where(small == p, top, stats)
            stats = jnp.where(small == GROUP + p, total, stats)
        row_ref[pl.ds(row, 16), :] = stats
        return carry

    lax.fori_loop(0, ROWS // 16, soft_rows, 0)
    for pair in range(3):
        st_ref[g, pair] = row_ref[pair * LANE : (pair + 1) * LANE, :].T[0:8, :]

    def one_out(p, carry):
        cols = pl.ds(pl.multiple_of((g * GROUP + p) * LANE, LANE), LANE)
        out = jnp.dot(probs_ref[p], v_ref[:, cols], preferred_element_type=F32)
        ob_ref[:, cols] = out.astype(BF16)
        return carry

    lax.fori_loop(0, GROUP, one_out, 0)


def combine_group(g, og_ref, sg_ref, out_ref):
    tiles = sg_ref[g].reshape(16 * 8, LANE).T
    parts = []
    for lag in range(SPAN):
        at = (lag % 2) * CHUNK
        part = tiles[at : at + CHUNK, :]
        parts.append(pltpu.roll(part, LANE - 8 * lag, 1) if lag else part)
    top = parts[0]
    for part in parts[1:]:
        top = jnp.maximum(top, part)
    scales = [jnp.exp(part - top) for part in parts]
    total = jnp.zeros((CHUNK, LANE), F32)
    for part, scale in zip(parts, scales):
        total = total + scale * pltpu.roll(part, LANE - GROUP, 1)
    for p in range(GROUP):
        cols = pl.ds(pl.multiple_of((g * GROUP + p) * LANE, LANE), LANE)
        acc = jnp.zeros((CHUNK, LANE), F32)
        for lag in range(SPAN):
            acc = acc + og_ref[lag, :, cols].astype(F32) * scales[lag][:, p : p + 1]
        out_ref[:, cols] = (acc / total[:, p : p + 1]).astype(BF16)


def kernel(
    q_hbm, k_hbm, v_hbm, cw_ref, mw_ref, doc_ref, out_ref,
    qg_ref, qh_ref, k_ref, v_ref, kn_ref, kt_ref, base_ref, w_ref, msc_ref,
    msk_ref, x_ref, conv_ref, probs_ref, row_ref, ob_ref, st_ref, og_ref, sg_ref, qr_ref, hr_ref,
    local_sem, q_send, q_recv, h_send, h_recv, n_send, n_recv, o_send, o_recv, s_send, s_recv,
    u_send, u_recv, v_send, v_recv,
):
    qb, kb = lax.axis_index("qb"), lax.axis_index("kb")
    mine = qb * 16 + kb
    after = mine + 1
    held = relayed(qb, kb)
    chunks = [served(qb, kb, lag) for lag in range(SPAN)]

    def is_me(where):
        return jnp.logical_and(where[0] == qb, where[1] == kb)

    def both(a, b):
        return jnp.logical_and(a, b)

    def place(where):
        return {"qb": where[0], "kb": where[1]}

    true = kb >= 0
    works = [kb + lag <= 15 for lag in range(SPAN)]
    sends = [mine // 8 >= lag for lag in range(SPAN)]
    hands = [held // 8 >= lag for lag in range(SPAN)]
    last = mine == 127
    first = held == 0
    halo_out, halo_in = jnp.logical_not(last), jnp.logical_not(first)

    load_k = pltpu.make_async_copy(k_hbm, k_ref, local_sem.at[0])
    load_v = pltpu.make_async_copy(v_hbm, v_ref, local_sem.at[1])
    load_k.start()
    load_v.start()

    @pl.when(kb == 0)
    def _():
        kn_ref[0] = jnp.zeros((16, WIDTH), BF16)

    @pl.when(kb == 15)
    def _():
        kn_ref[1] = jnp.zeros((16, WIDTH), BF16)

    @pl.when(first)
    def _():
        hr_ref[...] = jnp.zeros_like(hr_ref)

    for lag in range(1, SPAN):
        @pl.when(jnp.logical_not(sends[lag]))
        def _():
            og_ref[lag] = jnp.zeros((CHUNK, WIDTH), BF16)
    sg_ref[...] = jnp.full(sg_ref.shape, LOW, F32)

    barrier = pltpu.get_barrier_semaphore()
    peers = [
        ((qb, kb + 1), kb < 15), ((qb, kb - 1), kb > 0),
        (relay(mine), true), (owner(held), true),
        (relay(after), halo_out), (owner(held - 1), halo_in),
    ]
    for lag in range(SPAN):
        peers.append((worker(held, lag), hands[lag]))
        peers.append((relay(chunks[lag]), works[lag]))
        peers.append((owner(chunks[lag]), works[lag]))
        peers.append((worker(mine, lag), sends[lag]))
    count = jnp.int32(0)
    for where, ok in peers:
        go = both(ok, jnp.logical_not(is_me(where)))

        @pl.when(go)
        def _():
            pl.semaphore_signal(barrier, inc=1, device_id=place(where), device_id_type=MESH)

        count = count + go.astype(jnp.int32)

    build_masks(qb, kb, doc_ref, msc_ref)
    build_bands(cw_ref, base_ref, w_ref)
    pl.semaphore_wait(barrier, count)

    def remote(src, dst, send, recv, where):
        return pltpu.make_async_remote_copy(
            src_ref=src, dst_ref=dst, send_sem=send, recv_sem=recv,
            device_id=place(where), device_id_type=MESH,
        )

    def start(parts, where, ok):
        src, dst, send, recv = parts
        here = is_me(where)

        @pl.when(both(ok, jnp.logical_not(here)))
        def _():
            remote(src, dst, send, recv, where).start()

        @pl.when(both(ok, here))
        def _():
            pltpu.make_async_copy(src, dst, recv).start()

    def sent(parts, where, ok):
        src, dst, send, recv = parts

        @pl.when(both(ok, jnp.logical_not(is_me(where))))
        def _():
            remote(src, dst, send, recv, where).wait_send()

    def landed(parts, where, ok):
        src, dst, send, recv = parts
        here = is_me(where)

        @pl.when(both(ok, jnp.logical_not(here)))
        def _():
            remote(src, dst, send, recv, where).wait_recv()

        @pl.when(both(ok, here))
        def _():
            pltpu.make_async_copy(src, dst, recv).wait()

    def lanes(start, size):
        return pl.ds(pl.multiple_of(start * size, size), size)

    def up_parts(h):
        return q_hbm.at[:, lanes(h, LANE)], qr_ref.at[h], u_send.at[h], u_recv.at[h]

    def up_halo_parts(g):
        return (
            q_hbm.at[CHUNK - 8 : CHUNK, lanes(g, HALFW)], hr_ref.at[g], v_send.at[g], v_recv.at[g]
        )

    def chunk_parts(h, lag):
        return (
            qr_ref.at[h], qg_ref.at[h, lag * EXT + HALO : (lag + 1) * EXT, :],
            q_send.at[h, lag], q_recv.at[h, lag],
        )

    def halo_parts(g, lag):
        return hr_ref.at[g], qh_ref.at[g, lag], h_send.at[g, lag], h_recv.at[g, lag]

    def out_parts(g, lag):
        cols = lanes(g, HALFW)
        return (
            ob_ref.at[lag * CHUNK : (lag + 1) * CHUNK, cols], og_ref.at[lag, :, cols],
            o_send.at[g, lag], o_recv.at[g, lag],
        )

    def stat_parts(g, lag):
        return st_ref.at[g, lag // 2], sg_ref.at[g, lag], s_send.at[g, lag], s_recv.at[g, lag]

    edges = [
        ((k_hbm.at[BLOCK - 16 : BLOCK, :], kn_ref.at[0], n_send.at[0], n_recv.at[0]),
         (qb, kb + 1), kb < 15, (qb, kb - 1), kb > 0),
        ((k_hbm.at[0:16, :], kn_ref.at[1], n_send.at[1], n_recv.at[1]),
         (qb, kb - 1), kb > 0, (qb, kb + 1), kb < 15),
    ]
    for parts, where, ok, _, _ in edges:
        start(parts, where, ok)

    def up_group(g, carry):
        start(up_halo_parts(g), relay(after), halo_out)

        def up_head(p, carry):
            start(up_parts(g * GROUP + p), relay(mine), true)
            return carry

        return lax.fori_loop(0, GROUP, up_head, carry)

    lax.fori_loop(0, GROUPS, up_group, 0)

    load_k.wait()
    for parts, _, _, where, ok in edges:
        landed(parts, where, ok)
    build_edges(k_ref, kn_ref, kt_ref)
    load_v.wait()

    def hand_group(g, carry):
        landed(up_halo_parts(g), owner(held - 1), halo_in)
        for lag in range(SPAN):
            start(halo_parts(g, lag), worker(held, lag), hands[lag])

        def hand_head(p, carry):
            h = g * GROUP + p
            landed(up_parts(h), owner(held), true)
            for lag in range(SPAN):
                start(chunk_parts(h, lag), worker(held, lag), hands[lag])
            return carry

        return lax.fori_loop(0, GROUP, hand_head, carry)

    lax.fori_loop(0, GROUPS, hand_group, 0)

    def arrive(h):
        for lag in range(SPAN):
            landed(chunk_parts(h, lag), relay(chunks[lag]), works[lag])

    def one_group(g, carry):
        for lag in range(SPAN):
            landed(halo_parts(g, lag), relay(chunks[lag]), works[lag])
        attend_group(
            g, arrive, mw_ref, qg_ref, qh_ref, k_ref, v_ref, kt_ref, w_ref, msc_ref,
            (msk_ref, x_ref, conv_ref, probs_ref, row_ref), ob_ref, st_ref,
        )
        for lag in range(SPAN):
            start(stat_parts(g, lag), owner(chunks[lag]), works[lag])
            start(out_parts(g, lag), owner(chunks[lag]), works[lag])
        return carry

    lax.fori_loop(0, GROUPS, one_group, 0)

    def one_result(g, carry):
        for lag in range(SPAN):
            landed(stat_parts(g, lag), worker(mine, lag), sends[lag])
            landed(out_parts(g, lag), worker(mine, lag), sends[lag])
        combine_group(g, og_ref, sg_ref, out_ref)
        return carry

    lax.fori_loop(0, GROUPS, one_result, 0)

    for parts, where, ok, _, _ in edges:
        sent(parts, where, ok)

    def drain(g, carry):
        sent(up_halo_parts(g), relay(after), halo_out)
        for lag in range(SPAN):
            sent(halo_parts(g, lag), worker(held, lag), hands[lag])
            sent(stat_parts(g, lag), owner(chunks[lag]), works[lag])
            sent(out_parts(g, lag), owner(chunks[lag]), works[lag])

        def drain_head(p, carry):
            h = g * GROUP + p
            sent(up_parts(h), relay(mine), true)
            for lag in range(SPAN):
                sent(chunk_parts(h, lag), worker(held, lag), hands[lag])
            return carry

        return lax.fori_loop(0, GROUP, drain_head, carry)

    lax.fori_loop(0, GROUPS, drain, 0)


def body(queries, keys, values, conv_weight, mix_weight, doc_ids):
    docs = doc_ids.reshape(-1, LANE)
    taps = conv_weight.transpose(1, 0, 2)
    any_space = pl.BlockSpec(memory_space=pl.ANY)
    vmem = pl.BlockSpec(memory_space=pltpu.VMEM)
    dma = pltpu.SemaphoreType.DMA
    return pl.pallas_call(
        kernel,
        out_shape=jax.ShapeDtypeStruct((CHUNK, WIDTH), BF16),
        in_specs=[
            any_space, any_space, any_space, vmem, pl.BlockSpec(memory_space=pltpu.SMEM), vmem,
        ],
        out_specs=vmem,
        scratch_shapes=[
            pltpu.VMEM((HEADS, EROWS, LANE), BF16),
            pltpu.VMEM((GROUPS, SPAN, 8, HALFW), BF16),
            pltpu.VMEM((BLOCK, WIDTH), BF16),
            pltpu.VMEM((BLOCK, WIDTH), BF16),
            pltpu.VMEM((2, 16, WIDTH), BF16),
            pltpu.VMEM((2 * LANE, WIDTH), BF16),
            pltpu.VMEM((8 * LAGS, LANE), F32),
            pltpu.VMEM((HEADS, DEPTH, HALF), BF16),
            pltpu.VMEM((6, EROWS, LANE), F32),
            pltpu.VMEM((6, EROWS, LANE), F32),
            pltpu.VMEM((2 * ROWS, DEPTH), BF16),
            pltpu.VMEM((GROUP, 2 * ROWS, HALF), F32),
            pltpu.VMEM((GROUP, ROWS, BLOCK), BF16),
            pltpu.VMEM((3 * LANE, LANE), F32),
            pltpu.VMEM((ROWS, WIDTH), BF16),
            pltpu.VMEM((GROUPS, 3, 8, LANE), F32),
            pltpu.VMEM((SPAN, CHUNK, WIDTH), BF16),
            pltpu.VMEM((GROUPS, 16, 8, LANE), F32),
            pltpu.VMEM((HEADS, CHUNK, LANE), BF16),
            pltpu.VMEM((GROUPS, 8, HALFW), BF16),
            dma((2,)),
            dma((HEADS, SPAN)), dma((HEADS, SPAN)),
            dma((GROUPS, SPAN)), dma((GROUPS, SPAN)),
            dma((2,)), dma((2,)),
            dma((GROUPS, SPAN)), dma((GROUPS, SPAN)),
            dma((GROUPS, SPAN)), dma((GROUPS, SPAN)),
            dma((HEADS,)), dma((HEADS,)),
            dma((GROUPS,)), dma((GROUPS,)),
        ],
        compiler_params=pltpu.CompilerParams(collective_id=0, has_side_effects=True),
    )(queries, keys, values, taps, mix_weight, docs)


def solution(mesh):
    placed = (
        P(("ba", "qb", "kb"), None),
        P(("ba", "kb"), None),
        P(("ba", "kb"), None),
        P(),
        P(),
        P("ba"),
    )
    return jax.shard_map(
        body, mesh=mesh, in_specs=placed, out_specs=P(("ba", "qb", "kb"), None), check_vma=False
    )
```

```python
import math

import jax
import jax.numpy as jnp
from jax import lax
from jax.experimental import pallas as pl
from jax.experimental.pallas import tpu as pltpu
from jax.sharding import PartitionSpec as P

MESH = pl.DeviceIdType.MESH
F32 = jnp.float32
BF16 = jnp.bfloat16

CHUNK = 64
HALO = 16
EXT = CHUNK + HALO
SPAN = 5
BLOCK = 512
HALF = 256
LANE = 128
LAGS = 6
REACH = 11
SIDE = 5
HEADS = 8
GROUP = 4
GROUPS = 2
DEPTH = LAGS * HALF + LANE
ROWS = SPAN * CHUNK
EROWS = SPAN * EXT
HALFW = GROUP * LANE
LOW = -1e30
LOG2E = 1.4426950408889634
WIDTH = HEADS * LANE


def swap(code):
    return code % 2 * 2 + code // 2


def shift(group):
    return swap((group + 2) % 4) + 3 * plane(group)


def plane(group):
    return (group + 14) % 16 // 4


def column(chunk):
    return (chunk % 8 + 64 - shift(chunk // 8)) % 8


def worker(chunk, lag):
    return column(chunk), chunk // 8 - lag


def relay(chunk):
    return column(chunk), plane(chunk // 8) * 4 + chunk % 4


def owner(chunk):
    return chunk // 16, chunk % 16


def served(qb, kb, lag):
    group = kb + lag
    return group * 8 + (qb + shift(group)) % 8


def relayed(qb, kb):
    level = kb // 4
    code = (kb + 64 - qb - 3 * level) % 4
    group = (4 * level + 2 + swap(code)) % 16
    return group * 8 + (qb + code + 3 * level) % 8


def iota(shape, dim):
    return lax.broadcasted_iota(jnp.int32, shape, dim)


def dot_nt(a, b):
    return lax.dot_general(a, b, (((1,), (1,)), ((), ())), preferred_element_type=F32)


def build_masks(qb, kb, doc_ref, msc_ref):
    scale = 1.0 / math.sqrt(LANE)
    docs = doc_ref[...]
    starts = []
    for value in range(1, 8):
        below = (docs < value).astype(F32)
        below = jnp.sum(jnp.sum(below, axis=0, keepdims=True), axis=1, keepdims=True)
        starts.append(jnp.broadcast_to(below.astype(jnp.int32), (EXT, LANE)))
    lane = iota((EXT, LANE), 1)
    first = kb * BLOCK
    edge = lane % 16
    edge = jnp.where(edge < 8, edge - 8, edge + (HALF - 8))
    for lag in range(SPAN):
        row = served(qb, kb, lag) * CHUNK - HALO + iota((EXT, LANE), 0)
        low = jnp.zeros((EXT, LANE), jnp.int32)
        for start in starts:
            low = jnp.where(start <= row, start, low)
        for tile in range(6):
            if tile < 4:
                col = first + tile * LANE + lane
            else:
                col = first + (tile - 4) * HALF + edge
            good = (col >= low) & (col <= row)
            msc_ref[tile, lag * EXT : (lag + 1) * EXT, :] = jnp.where(good, scale, 0.0).astype(F32)


def build_bands(cw_ref, base_ref, w_ref):
    base_ref[...] = jnp.zeros_like(base_ref)
    center = (iota((HEADS, REACH), 1) == REACH // 2).astype(F32)
    for a in range(LAGS):
        taps = cw_ref[a].astype(F32)
        base_ref[8 * a : 8 * a + HEADS, 0:REACH] = taps + center if a == 0 else taps
    base_ref[...] = pltpu.roll(base_ref[...], LANE - SIDE, 1)
    w_ref[...] = jnp.zeros_like(w_ref)
    diff = iota((LANE, LANE), 1) - iota((LANE, LANE), 0)
    near = (diff <= SIDE) & (diff >= -SIDE)
    blank = jnp.zeros((8, LANE), F32)

    def one_head(h, carry):
        for a in range(LAGS):
            ring = jnp.broadcast_to(base_ref[pl.ds(8 * a + h, 1), :], (LANE, LANE))
            ring = pltpu.roll(ring, 0, 1, stride=1, stride_axis=0)
            diag = jnp.where(near, ring, 0.0).astype(BF16)
            upper = jnp.where(diff[LANE - 8 :] <= SIDE - LANE, ring[LANE - 8 :], 0.0)
            lower = jnp.where(diff[:8] >= LANE - SIDE, ring[:8], 0.0)
            top = a * HALF
            w_ref[h, top : top + LANE, 0:LANE] = diag
            w_ref[h, top + LANE : top + HALF, LANE:HALF] = diag
            w_ref[h, top + LANE - 16 : top + LANE, LANE:HALF] = jnp.concatenate(
                [blank, upper], axis=0
            ).astype(BF16)
            w_ref[h, top + LANE : top + LANE + 16, 0:LANE] = jnp.concatenate(
                [lower, blank], axis=0
            ).astype(BF16)
            edge = LAGS * HALF + 16 * a
            w_ref[h, edge : edge + 16, 0:LANE] = jnp.concatenate([upper, blank], axis=0).astype(BF16)
            w_ref[h, edge : edge + 16, LANE:HALF] = jnp.concatenate(
                [blank, lower], axis=0
            ).astype(BF16)
        return carry

    lax.fori_loop(0, HEADS, one_head, 0)


def build_edges(k_ref, kn_ref, kt_ref):
    left = [kn_ref[0], k_ref[HALF - 16 : HALF, :]]
    right = [k_ref[HALF : HALF + 16, :], kn_ref[1]]
    for t in range(2):
        pair = jnp.concatenate([left[t].astype(F32)[8:16], right[t].astype(F32)[0:8]], axis=0)
        pair = pair.astype(BF16)
        for a in range(8):
            kt_ref[t * LANE + 16 * a : t * LANE + 16 * a + 16, :] = pair


def attend_group(
    g, arrive, leave, mw_ref, qg_ref, qh_ref, k_ref, v_ref, kt_ref, w_ref, msc_ref, scratch, ob_ref, st_ref
):
    msk_ref, x_ref, conv_ref, probs_ref, row_ref = scratch
    lane = iota((CHUNK, LANE), 1)

    def one_head(p, carry):
        h = g * GROUP + p
        cols = pl.ds(pl.multiple_of(h * LANE, LANE), LANE)
        arrive(h)
        for lag in range(SPAN):
            edge = qh_ref[g, lag, :, pl.ds(pl.multiple_of(p * LANE, LANE), LANE)].astype(F32)
            edge = jnp.concatenate([edge, edge], axis=0).astype(BF16)
            qg_ref[h, lag * EXT : lag * EXT + HALO, :] = edge
        q = qg_ref[h]
        for t in range(3):
            keys = k_ref[t * HALF : (t + 1) * HALF, cols] if t < 2 else kt_ref[:, cols]
            logits = dot_nt(q, keys)
            for u in range(2):
                msk_ref[2 * t + u] = logits[:, u * LANE : (u + 1) * LANE] * msc_ref[2 * t + u]
        for lag in range(SPAN):
            base = lag * EXT + HALO
            for t in range(2):
                to = t * ROWS + lag * CHUNK
                for a in range(LAGS):
                    for u in range(2):
                        piece = msk_ref[2 * t + u, base - a : base - a + CHUNK, :]
                        at = a * HALF + u * LANE
                        x_ref[to : to + CHUNK, at : at + LANE] = piece.astype(BF16)
                piece = msk_ref[4 + t, base : base + CHUNK, :]
                for a in range(1, LAGS):
                    other = msk_ref[4 + t, base - a : base - a + CHUNK, :]
                    piece = jnp.where(lane >= 16 * a, other, piece)
                x_ref[to : to + CHUNK, LAGS * HALF : DEPTH] = piece.astype(BF16)
        conv_ref[p] = jnp.dot(x_ref[...], w_ref[h], preferred_element_type=F32)
        return carry

    lax.fori_loop(0, GROUP, one_head, 0)
    weights = [
        [(mw_ref[g, p, q] + (1.0 if p == q else 0.0)) * LOG2E for q in range(GROUP)] for p in range(GROUP)
    ]
    small = iota((16, LANE), 1)

    def one_lag(lag, carry):
        for b in range(CHUNK // 16):
            row = pl.multiple_of(lag * CHUNK + b * 16, 16)
            erow = pl.multiple_of(lag * EXT + HALO + b * 16, 16)
            good = [msc_ref[tile, pl.ds(erow, 16), :] > 0 for tile in range(4)]
            conv = [
                [
                    conv_ref[q, pl.ds(pl.multiple_of((tile // 2) * ROWS + row, 16), 16),
                             (tile % 2) * LANE : (tile % 2 + 1) * LANE]
                    for tile in range(4)
                ]
                for q in range(GROUP)
            ]
            stats = jnp.zeros((16, LANE), F32)
            for p in range(GROUP):
                mixed = []
                for tile in range(4):
                    total = conv[0][tile] * weights[p][0]
                    for q in range(1, GROUP):
                        total = total + conv[q][tile] * weights[p][q]
                    mixed.append(jnp.where(good[tile], total, LOW))
                top = jnp.maximum(
                    jnp.maximum(mixed[0], mixed[1]), jnp.maximum(mixed[2], mixed[3])
                )
                top = jnp.max(top, axis=1, keepdims=True)
                expo = [jnp.exp2(m - top) for m in mixed]
                for tile in range(4):
                    probs_ref[p, b * 16 : b * 16 + 16, tile * LANE : (tile + 1) * LANE] = expo[
                        tile
                    ].astype(BF16)
                total = jnp.sum(
                    (expo[0] + expo[1]) + (expo[2] + expo[3]), axis=1, keepdims=True
                )
                stats = jnp.where(small == p, top, stats)
                stats = jnp.where(small == GROUP + p, total, stats)
            row_ref[b * 16 : b * 16 + 16, :] = stats
        st_ref[g, lag] = row_ref[...].T[0:8, :]
        for p in range(GROUP):
            cols = pl.ds(pl.multiple_of((g * GROUP + p) * LANE, LANE), LANE)
            out = jnp.dot(probs_ref[p], v_ref[:, cols], preferred_element_type=F32)
            ob_ref[lag, :, cols] = out.astype(BF16)
        leave(lag)
        return carry

    lax.fori_loop(0, SPAN, one_lag, 0)


def combine_group(g, og_ref, sg_ref, out_ref):
    tiles = sg_ref[g].reshape(16 * 8, LANE).T[:CHUNK]
    parts = [
        pltpu.roll(tiles, LANE - 8 * lag, 1) if lag else tiles for lag in range(SPAN)
    ]
    top = parts[0]
    for part in parts[1:]:
        top = jnp.maximum(top, part)
    scales = [jnp.exp2(part - top) for part in parts]
    total = jnp.zeros((CHUNK, LANE), F32)
    for part, scale in zip(parts, scales):
        total = total + scale * pltpu.roll(part, LANE - GROUP, 1)
    for p in range(GROUP):
        cols = pl.ds(pl.multiple_of((g * GROUP + p) * LANE, LANE), LANE)
        acc = jnp.zeros((CHUNK, LANE), F32)
        for lag in range(SPAN):
            acc = acc + og_ref[lag, :, cols].astype(F32) * scales[lag][:, p : p + 1]
        out_ref[:, cols] = (acc / total[:, p : p + 1]).astype(BF16)


def kernel(
    q_hbm, k_hbm, v_hbm, cw_ref, mw_ref, doc_ref, out_ref,
    qg_ref, qh_ref, k_ref, v_ref, kn_ref, kt_ref, base_ref, w_ref, msc_ref,
    msk_ref, x_ref, conv_ref, probs_ref, row_ref, ob_ref, st_ref, og_ref, sg_ref, qr_ref, hr_ref,
    local_sem, q_send, q_recv, h_send, h_recv, n_send, n_recv, o_send, o_recv, s_send, s_recv,
    u_send, u_recv, v_send, v_recv,
):
    qb, kb = lax.axis_index("qb"), lax.axis_index("kb")
    mine = qb * 16 + kb
    after = mine + 1
    held = relayed(qb, kb)
    chunks = [served(qb, kb, lag) for lag in range(SPAN)]

    def is_me(where):
        return jnp.logical_and(where[0] == qb, where[1] == kb)

    def both(a, b):
        return jnp.logical_and(a, b)

    def place(where):
        return {"qb": where[0], "kb": where[1]}

    true = kb >= 0
    works = [kb + lag <= 15 for lag in range(SPAN)]
    sends = [mine // 8 >= lag for lag in range(SPAN)]
    hands = [held // 8 >= lag for lag in range(SPAN)]
    last = mine == 127
    first = held == 0
    halo_out, halo_in = jnp.logical_not(last), jnp.logical_not(first)

    barrier = pltpu.get_barrier_semaphore()

    def greet(where, ok):
        @pl.when(both(ok, jnp.logical_not(is_me(where))))
        def _():
            pl.semaphore_signal(barrier, inc=1, device_id=place(where), device_id_type=MESH)

    greet((qb, kb + 1), kb < 15)
    greet((qb, kb - 1), kb > 0)
    greet(owner(held), true)
    greet(owner(held - 1), halo_in)
    for lag in range(SPAN):
        greet(relay(chunks[lag]), works[lag])
    senders = [
        ((qb, kb + 1), kb < 15), ((qb, kb - 1), kb > 0),
        (relay(mine), true), (relay(after), halo_out),
    ]
    senders += [(worker(held, lag), hands[lag]) for lag in range(SPAN)]
    count = jnp.int32(0)
    for where, ok in senders:
        count = count + both(ok, jnp.logical_not(is_me(where))).astype(jnp.int32)

    load_k = pltpu.make_async_copy(k_hbm, k_ref, local_sem.at[0])
    load_v = pltpu.make_async_copy(v_hbm, v_ref, local_sem.at[1])
    load_k.start()
    load_v.start()

    @pl.when(kb == 0)
    def _():
        kn_ref[0] = jnp.zeros((16, WIDTH), BF16)

    @pl.when(kb == 15)
    def _():
        kn_ref[1] = jnp.zeros((16, WIDTH), BF16)

    @pl.when(first)
    def _():
        hr_ref[...] = jnp.zeros_like(hr_ref)

    for lag in range(1, SPAN):
        @pl.when(jnp.logical_not(sends[lag]))
        def _():
            og_ref[lag] = jnp.zeros((CHUNK, WIDTH), BF16)
    sg_ref[...] = jnp.full(sg_ref.shape, LOW, F32)

    build_masks(qb, kb, doc_ref, msc_ref)
    build_bands(cw_ref, base_ref, w_ref)
    pl.semaphore_wait(barrier, count)

    def remote(src, dst, send, recv, where):
        return pltpu.make_async_remote_copy(
            src_ref=src, dst_ref=dst, send_sem=send, recv_sem=recv,
            device_id=place(where), device_id_type=MESH,
        )

    def start(parts, where, ok):
        src, dst, send, recv = parts
        here = is_me(where)

        @pl.when(both(ok, jnp.logical_not(here)))
        def _():
            remote(src, dst, send, recv, where).start()

        @pl.when(both(ok, here))
        def _():
            pltpu.make_async_copy(src, dst, recv).start()

    def sent(parts, where, ok):
        src, dst, send, recv = parts

        @pl.when(both(ok, jnp.logical_not(is_me(where))))
        def _():
            remote(src, dst, send, recv, where).wait_send()

    def landed(parts, where, ok):
        src, dst, send, recv = parts
        here = is_me(where)

        @pl.when(both(ok, jnp.logical_not(here)))
        def _():
            remote(src, dst, send, recv, where).wait_recv()

        @pl.when(both(ok, here))
        def _():
            pltpu.make_async_copy(src, dst, recv).wait()

    def lanes(start, size):
        return pl.ds(pl.multiple_of(start * size, size), size)

    def up_parts(h):
        return q_hbm.at[:, lanes(h, LANE)], qr_ref.at[h], u_send.at[h], u_recv.at[h]

    def up_halo_parts(g):
        return (
            q_hbm.at[CHUNK - 8 : CHUNK, lanes(g, HALFW)], hr_ref.at[g], v_send.at[g], v_recv.at[g]
        )

    def chunk_parts(h, lag):
        return (
            qr_ref.at[h], qg_ref.at[h, lag * EXT + HALO : (lag + 1) * EXT, :],
            q_send.at[h, lag], q_recv.at[h, lag],
        )

    def halo_parts(g, lag):
        return hr_ref.at[g], qh_ref.at[g, lag], h_send.at[g, lag], h_recv.at[g, lag]

    def out_parts(g, lag):
        cols = lanes(g, HALFW)
        return (
            ob_ref.at[lag, :, cols], og_ref.at[lag, :, cols],
            o_send.at[g, lag], o_recv.at[g, lag],
        )

    def stat_parts(g, lag):
        return st_ref.at[g, lag], sg_ref.at[g, lag], s_send.at[g, lag], s_recv.at[g, lag]

    edges = [
        ((k_hbm.at[BLOCK - 16 : BLOCK, :], kn_ref.at[0], n_send.at[0], n_recv.at[0]),
         (qb, kb + 1), kb < 15, (qb, kb - 1), kb > 0),
        ((k_hbm.at[0:16, :], kn_ref.at[1], n_send.at[1], n_recv.at[1]),
         (qb, kb - 1), kb > 0, (qb, kb + 1), kb < 15),
    ]
    for parts, where, ok, _, _ in edges:
        start(parts, where, ok)

    def up_group(g, carry):
        start(up_halo_parts(g), relay(after), halo_out)

        def up_head(p, carry):
            start(up_parts(g * GROUP + p), relay(mine), true)
            return carry

        return lax.fori_loop(0, GROUP, up_head, carry)

    lax.fori_loop(0, GROUPS, up_group, 0)

    load_k.wait()
    for parts, _, _, where, ok in edges:
        landed(parts, where, ok)
    build_edges(k_ref, kn_ref, kt_ref)
    load_v.wait()

    def hand_group(g, carry):
        landed(up_halo_parts(g), owner(held - 1), halo_in)
        for lag in range(SPAN):
            start(halo_parts(g, lag), worker(held, lag), hands[lag])

        def hand_head(p, carry):
            h = g * GROUP + p
            landed(up_parts(h), owner(held), true)
            for lag in range(SPAN):
                start(chunk_parts(h, lag), worker(held, lag), hands[lag])
            return carry

        return lax.fori_loop(0, GROUP, hand_head, carry)

    lax.fori_loop(0, GROUPS, hand_group, 0)

    def arrive(h):
        for lag in range(SPAN):
            landed(chunk_parts(h, lag), relay(chunks[lag]), works[lag])

    def one_group(g, carry):
        for lag in range(SPAN):
            landed(halo_parts(g, lag), relay(chunks[lag]), works[lag])

        def leave(lag):
            where, ok = owner(served(qb, kb, lag)), kb + lag <= 15
            start(stat_parts(g, lag), where, ok)
            start(out_parts(g, lag), where, ok)

        attend_group(
            g, arrive, leave, mw_ref, qg_ref, qh_ref, k_ref, v_ref, kt_ref, w_ref, msc_ref,
            (msk_ref, x_ref, conv_ref, probs_ref, row_ref), ob_ref, st_ref,
        )
        return carry

    lax.fori_loop(0, GROUPS, one_group, 0)

    def one_result(g, carry):
        for lag in range(SPAN):
            landed(stat_parts(g, lag), worker(mine, lag), sends[lag])
            landed(out_parts(g, lag), worker(mine, lag), sends[lag])
        combine_group(g, og_ref, sg_ref, out_ref)
        return carry

    lax.fori_loop(0, GROUPS, one_result, 0)

    for parts, where, ok, _, _ in edges:
        sent(parts, where, ok)

    def drain(g, carry):
        sent(up_halo_parts(g), relay(after), halo_out)
        for lag in range(SPAN):
            sent(halo_parts(g, lag), worker(held, lag), hands[lag])
            sent(stat_parts(g, lag), owner(chunks[lag]), works[lag])
            sent(out_parts(g, lag), owner(chunks[lag]), works[lag])

        def drain_head(p, carry):
            h = g * GROUP + p
            sent(up_parts(h), relay(mine), true)
            for lag in range(SPAN):
                sent(chunk_parts(h, lag), worker(held, lag), hands[lag])
            return carry

        return lax.fori_loop(0, GROUP, drain_head, carry)

    lax.fori_loop(0, GROUPS, drain, 0)


def body(queries, keys, values, conv_weight, mix_weight, doc_ids):
    docs = doc_ids.reshape(-1, LANE)
    taps = conv_weight.transpose(1, 0, 2)
    any_space = pl.BlockSpec(memory_space=pl.ANY)
    vmem = pl.BlockSpec(memory_space=pltpu.VMEM)
    dma = pltpu.SemaphoreType.DMA
    return pl.pallas_call(
        kernel,
        out_shape=jax.ShapeDtypeStruct((CHUNK, WIDTH), BF16),
        in_specs=[
            any_space, any_space, any_space, vmem, pl.BlockSpec(memory_space=pltpu.SMEM), vmem,
        ],
        out_specs=vmem,
        scratch_shapes=[
            pltpu.VMEM((HEADS, EROWS, LANE), BF16),
            pltpu.VMEM((GROUPS, SPAN, 8, HALFW), BF16),
            pltpu.VMEM((BLOCK, WIDTH), BF16),
            pltpu.VMEM((BLOCK, WIDTH), BF16),
            pltpu.VMEM((2, 16, WIDTH), BF16),
            pltpu.VMEM((2 * LANE, WIDTH), BF16),
            pltpu.VMEM((8 * LAGS, LANE), F32),
            pltpu.VMEM((HEADS, DEPTH, HALF), BF16),
            pltpu.VMEM((6, EROWS, LANE), F32),
            pltpu.VMEM((6, EROWS, LANE), F32),
            pltpu.VMEM((2 * ROWS, DEPTH), BF16),
            pltpu.VMEM((GROUP, 2 * ROWS, HALF), F32),
            pltpu.VMEM((GROUP, CHUNK, BLOCK), BF16),
            pltpu.VMEM((LANE, LANE), F32),
            pltpu.VMEM((SPAN, CHUNK, WIDTH), BF16),
            pltpu.VMEM((GROUPS, SPAN, 8, LANE), F32),
            pltpu.VMEM((SPAN, CHUNK, WIDTH), BF16),
            pltpu.VMEM((GROUPS, 16, 8, LANE), F32),
            pltpu.VMEM((HEADS, CHUNK, LANE), BF16),
            pltpu.VMEM((GROUPS, 8, HALFW), BF16),
            dma((2,)),
            dma((HEADS, SPAN)), dma((HEADS, SPAN)),
            dma((GROUPS, SPAN)), dma((GROUPS, SPAN)),
            dma((2,)), dma((2,)),
            dma((GROUPS, SPAN)), dma((GROUPS, SPAN)),
            dma((GROUPS, SPAN)), dma((GROUPS, SPAN)),
            dma((HEADS,)), dma((HEADS,)),
            dma((GROUPS,)), dma((GROUPS,)),
        ],
        compiler_params=pltpu.CompilerParams(collective_id=0, has_side_effects=True),
    )(queries, keys, values, taps, mix_weight, docs)


def solution(mesh):
    placed = (
        P(("ba", "qb", "kb"), None),
        P(("ba", "kb"), None),
        P(("ba", "kb"), None),
        P(),
        P(),
        P("ba"),
    )
    return jax.shard_map(
        body, mesh=mesh, in_specs=placed, out_specs=P(("ba", "qb", "kb"), None), check_vma=False
    )
```

```python
import math

import jax
import jax.numpy as jnp
from jax import lax
from jax.experimental import pallas as pl
from jax.experimental.pallas import tpu as pltpu
from jax.sharding import PartitionSpec as P

MESH = pl.DeviceIdType.MESH
F32 = jnp.float32
BF16 = jnp.bfloat16

CHUNK = 64
HALO = 16
EXT = CHUNK + HALO
SPAN = 5
BLOCK = 512
HALF = 256
LANE = 128
LAGS = 6
REACH = 11
SIDE = 5
HEADS = 8
GROUP = 4
GROUPS = 2
TILES = BLOCK // LANE
PAIRS = CHUNK // 2
READS = LAGS + 1
DEPTH = READS * LANE + LANE
ROWS = SPAN * CHUNK
EROWS = SPAN * EXT
HALFW = GROUP * LANE
LOW = -1e30
LOG2E = 1.4426950408889634
WIDTH = HEADS * LANE


def swap(code):
    return code % 2 * 2 + code // 2


def shift(group):
    return swap((group + 2) % 4) + 3 * plane(group)


def plane(group):
    return (group + 14) % 16 // 4


def column(chunk):
    return (chunk % 8 + 64 - shift(chunk // 8)) % 8


def worker(chunk, lag):
    return column(chunk), chunk // 8 - lag


def relay(chunk):
    return column(chunk), plane(chunk // 8) * 4 + chunk % 4


def owner(chunk):
    return chunk // 16, chunk % 16


def served(qb, kb, lag):
    group = kb + lag
    return group * 8 + (qb + shift(group)) % 8


def relayed(qb, kb):
    level = kb // 4
    code = (kb + 64 - qb - 3 * level) % 4
    group = (4 * level + 2 + swap(code)) % 16
    return group * 8 + (qb + code + 3 * level) % 8


def iota(shape, dim):
    return lax.broadcasted_iota(jnp.int32, shape, dim)


def dot_nt(a, b):
    return lax.dot_general(a, b, (((1,), (1,)), ((), ())), preferred_element_type=F32)


def build_masks(qb, kb, doc_ref, msc_ref):
    scale = 1.0 / math.sqrt(LANE)
    docs = doc_ref[...]
    starts = []
    for value in range(1, 8):
        below = (docs < value).astype(F32)
        below = jnp.sum(jnp.sum(below, axis=0, keepdims=True), axis=1, keepdims=True)
        starts.append(jnp.broadcast_to(below.astype(jnp.int32), (EXT, LANE)))
    lane = iota((EXT, LANE), 1)
    first = kb * BLOCK
    edge = lane % 16
    edge = jnp.where(edge < 8, edge - 8, edge + (LANE - 8))
    for lag in range(SPAN):
        row = served(qb, kb, lag) * CHUNK - HALO + iota((EXT, LANE), 0)
        low = jnp.zeros((EXT, LANE), jnp.int32)
        for start in starts:
            low = jnp.where(start <= row, start, low)
        for tile in range(2 * TILES):
            if tile < TILES:
                col = first + tile * LANE + lane
            else:
                col = first + (tile - TILES) * LANE + edge
            good = (col >= low) & (col <= row)
            msc_ref[tile, lag * EXT : (lag + 1) * EXT, :] = jnp.where(good, scale, 0.0).astype(F32)


def build_bands(cw_ref, base_ref, w_ref):
    base_ref[...] = jnp.zeros_like(base_ref)
    center = (iota((HEADS, REACH), 1) == REACH // 2).astype(F32)
    for a in range(LAGS):
        taps = cw_ref[a].astype(F32)
        base_ref[8 * a : 8 * a + HEADS, 0:REACH] = taps + center if a == 0 else taps
    base_ref[...] = pltpu.roll(base_ref[...], LANE - SIDE, 1)
    w_ref[...] = jnp.zeros_like(w_ref)
    diff = iota((LANE, LANE), 1) - iota((LANE, LANE), 0)
    near = (diff <= SIDE) & (diff >= -SIDE)

    def one_head(h, carry):
        for a in range(LAGS):
            ring = jnp.broadcast_to(base_ref[pl.ds(8 * a + h, 1), :], (LANE, LANE))
            ring = pltpu.roll(ring, 0, 1, stride=1, stride_axis=0)
            diag = jnp.where(near, ring, 0.0).astype(BF16)
            upper = jnp.where(diff[LANE - 8 :] <= SIDE - LANE, ring[LANE - 8 :], 0.0)
            lower = jnp.where(diff[:8] >= LANE - SIDE, ring[:8], 0.0)
            rim = jnp.concatenate([upper, lower], axis=0).astype(BF16)
            for e in range(2):
                read = LAGS - 1 - a + e
                edge = READS * LANE + 16 * read
                w_ref[h, read * LANE : (read + 1) * LANE, e * LANE : (e + 1) * LANE] = diag
                w_ref[h, edge : edge + 16, e * LANE : (e + 1) * LANE] = rim
        return carry

    lax.fori_loop(0, HEADS, one_head, 0)


def build_edges(k_ref, kn_ref, kt_ref):
    for t in range(TILES):
        left = k_ref[t * LANE - 16 : t * LANE, :] if t else kn_ref[0]
        right = k_ref[(t + 1) * LANE : (t + 1) * LANE + 16, :] if t < TILES - 1 else kn_ref[1]
        pair = jnp.concatenate([left.astype(F32)[8:16], right.astype(F32)[0:8]], axis=0)
        pair = pair.astype(BF16)
        for a in range(8):
            kt_ref[t * LANE + 16 * a : t * LANE + 16 * a + 16, :] = pair


def attend_group(
    g, arrive, leave, mw_ref, qg_ref, qh_ref, k_ref, v_ref, kt_ref, w_ref, msc_ref, scratch, ob_ref, st_ref
):
    msk_ref, x_ref, conv_ref, probs_ref, row_ref = scratch
    lane = iota((PAIRS, LANE), 1)

    def one_head(p, carry):
        h = g * GROUP + p
        cols = pl.ds(pl.multiple_of(h * LANE, LANE), LANE)
        arrive(h)
        for lag in range(SPAN):
            edge = qh_ref[g, lag, :, pl.ds(pl.multiple_of(p * LANE, LANE), LANE)].astype(F32)
            edge = jnp.concatenate([edge, edge], axis=0).astype(BF16)
            qg_ref[h, lag * EXT : lag * EXT + HALO, :] = edge
        q = qg_ref[h]
        for t in range(TILES):
            part = (t % 2) * HALF
            keys = k_ref[part : part + HALF, cols] if t < 2 else kt_ref[part : part + HALF, cols]
            logits = dot_nt(q, keys)
            for u in range(2):
                msk_ref[2 * t + u] = logits[:, u * LANE : (u + 1) * LANE] * msc_ref[2 * t + u]
        for lag in range(SPAN):
            base = lag * EXT + HALO - (LAGS - 1)
            for t in range(TILES):
                to = (t * SPAN + lag) * PAIRS
                rim = msk_ref[TILES + t, pl.ds(base, PAIRS, stride=2), :]
                for read in range(READS):
                    piece = msk_ref[t, pl.ds(base + read, PAIRS, stride=2), :]
                    x_ref[to : to + PAIRS, read * LANE : (read + 1) * LANE] = piece.astype(BF16)
                    if read:
                        other = msk_ref[TILES + t, pl.ds(base + read, PAIRS, stride=2), :]
                        rim = jnp.where(lane >= 16 * read, other, rim)
                x_ref[to : to + PAIRS, READS * LANE : DEPTH] = rim.astype(BF16)
        conv_ref[p] = jnp.dot(x_ref[...], w_ref[h], preferred_element_type=F32)
        return carry

    lax.fori_loop(0, GROUP, one_head, 0)
    weights = [
        [(mw_ref[g, p, q] + (1.0 if p == q else 0.0)) * LOG2E for q in range(GROUP)] for p in range(GROUP)
    ]
    small = iota((16, LANE), 1)

    def one_lag(lag, carry):
        for b in range(CHUNK // 16):
            parity, half = b // 2, b % 2
            good = [
                msc_ref[tile, pl.ds(lag * EXT + HALO + half * 32 + parity, 16, stride=2), :] > 0
                for tile in range(TILES)
            ]
            conv = [
                [
                    conv_ref[
                        q,
                        pl.ds(pl.multiple_of((tile * SPAN + lag) * PAIRS + half * 16, 16), 16),
                        parity * LANE : (parity + 1) * LANE,
                    ]
                    for tile in range(TILES)
                ]
                for q in range(GROUP)
            ]
            stats = jnp.zeros((16, LANE), F32)
            for p in range(GROUP):
                mixed = []
                for tile in range(4):
                    total = conv[0][tile] * weights[p][0]
                    for q in range(1, GROUP):
                        total = total + conv[q][tile] * weights[p][q]
                    mixed.append(jnp.where(good[tile], total, LOW))
                top = jnp.maximum(
                    jnp.maximum(mixed[0], mixed[1]), jnp.maximum(mixed[2], mixed[3])
                )
                top = jnp.max(top, axis=1, keepdims=True)
                expo = [jnp.exp2(m - top) for m in mixed]
                for tile in range(4):
                    probs_ref[p, b * 16 : b * 16 + 16, tile * LANE : (tile + 1) * LANE] = expo[
                        tile
                    ].astype(BF16)
                total = jnp.sum(
                    (expo[0] + expo[1]) + (expo[2] + expo[3]), axis=1, keepdims=True
                )
                stats = jnp.where(small == p, top, stats)
                stats = jnp.where(small == GROUP + p, total, stats)
            row_ref[b * 16 : b * 16 + 16, :] = stats
        st_ref[g, lag] = row_ref[...].T[0:8, :]
        for p in range(GROUP):
            cols = pl.ds(pl.multiple_of((g * GROUP + p) * LANE, LANE), LANE)
            out = jnp.dot(probs_ref[p], v_ref[:, cols], preferred_element_type=F32)
            ob_ref[lag, :, cols] = out.astype(BF16)
        leave(lag)
        return carry

    lax.fori_loop(0, SPAN, one_lag, 0)


def combine_group(g, og_ref, sg_ref, fin_ref, out_ref):
    tiles = sg_ref[g].reshape(16 * 8, LANE).T[:CHUNK]
    parts = [
        pltpu.roll(tiles, LANE - 8 * lag, 1) if lag else tiles for lag in range(SPAN)
    ]
    top = parts[0]
    for part in parts[1:]:
        top = jnp.maximum(top, part)
    scales = [jnp.exp2(part - top) for part in parts]
    total = jnp.zeros((CHUNK, LANE), F32)
    for part, scale in zip(parts, scales):
        total = total + scale * pltpu.roll(part, LANE - GROUP, 1)
    for p in range(GROUP):
        cols = pl.ds(pl.multiple_of((g * GROUP + p) * LANE, LANE), LANE)
        acc = jnp.zeros((CHUNK, LANE), F32)
        for lag in range(SPAN):
            acc = acc + og_ref[lag, :, cols].astype(F32) * scales[lag][:, p : p + 1]
        acc = acc / total[:, p : p + 1]
        for parity in range(2):
            fin_ref[p, pl.ds(parity, PAIRS, stride=2), :] = acc[
                parity * PAIRS : (parity + 1) * PAIRS
            ]
        out_ref[:, cols] = fin_ref[p].astype(BF16)


def kernel(
    q_hbm, k_hbm, v_hbm, cw_ref, mw_ref, doc_ref, out_ref,
    qg_ref, qh_ref, k_ref, v_ref, kn_ref, kt_ref, base_ref, w_ref, msc_ref,
    msk_ref, x_ref, conv_ref, probs_ref, row_ref, ob_ref, st_ref, og_ref, sg_ref, fin_ref, qr_ref, hr_ref,
    local_sem, q_send, q_recv, h_send, h_recv, n_send, n_recv, o_send, o_recv, s_send, s_recv,
    u_send, u_recv, v_send, v_recv,
):
    qb, kb = lax.axis_index("qb"), lax.axis_index("kb")
    mine = qb * 16 + kb
    after = mine + 1
    held = relayed(qb, kb)
    chunks = [served(qb, kb, lag) for lag in range(SPAN)]

    def is_me(where):
        return jnp.logical_and(where[0] == qb, where[1] == kb)

    def both(a, b):
        return jnp.logical_and(a, b)

    def place(where):
        return {"qb": where[0], "kb": where[1]}

    true = kb >= 0
    works = [kb + lag <= 15 for lag in range(SPAN)]
    sends = [mine // 8 >= lag for lag in range(SPAN)]
    hands = [held // 8 >= lag for lag in range(SPAN)]
    last = mine == 127
    first = held == 0
    halo_out, halo_in = jnp.logical_not(last), jnp.logical_not(first)

    barrier = pltpu.get_barrier_semaphore()

    def greet(where, ok):
        @pl.when(both(ok, jnp.logical_not(is_me(where))))
        def _():
            pl.semaphore_signal(barrier, inc=1, device_id=place(where), device_id_type=MESH)

    greet((qb, kb + 1), kb < 15)
    greet((qb, kb - 1), kb > 0)
    greet(owner(held), true)
    greet(owner(held - 1), halo_in)
    for lag in range(SPAN):
        greet(relay(chunks[lag]), works[lag])
    senders = [
        ((qb, kb + 1), kb < 15), ((qb, kb - 1), kb > 0),
        (relay(mine), true), (relay(after), halo_out),
    ]
    senders += [(worker(held, lag), hands[lag]) for lag in range(SPAN)]
    count = jnp.int32(0)
    for where, ok in senders:
        count = count + both(ok, jnp.logical_not(is_me(where))).astype(jnp.int32)

    load_k = pltpu.make_async_copy(k_hbm, k_ref, local_sem.at[0])
    load_v = pltpu.make_async_copy(v_hbm, v_ref, local_sem.at[1])
    load_k.start()
    load_v.start()

    @pl.when(kb == 0)
    def _():
        kn_ref[0] = jnp.zeros((16, WIDTH), BF16)

    @pl.when(kb == 15)
    def _():
        kn_ref[1] = jnp.zeros((16, WIDTH), BF16)

    @pl.when(first)
    def _():
        hr_ref[...] = jnp.zeros_like(hr_ref)

    for lag in range(1, SPAN):
        @pl.when(jnp.logical_not(sends[lag]))
        def _():
            og_ref[lag] = jnp.zeros((CHUNK, WIDTH), BF16)
    sg_ref[...] = jnp.full(sg_ref.shape, LOW, F32)

    build_masks(qb, kb, doc_ref, msc_ref)
    build_bands(cw_ref, base_ref, w_ref)
    pl.semaphore_wait(barrier, count)

    def remote(src, dst, send, recv, where):
        return pltpu.make_async_remote_copy(
            src_ref=src, dst_ref=dst, send_sem=send, recv_sem=recv,
            device_id=place(where), device_id_type=MESH,
        )

    def start(parts, where, ok):
        src, dst, send, recv = parts
        here = is_me(where)

        @pl.when(both(ok, jnp.logical_not(here)))
        def _():
            remote(src, dst, send, recv, where).start()

        @pl.when(both(ok, here))
        def _():
            pltpu.make_async_copy(src, dst, recv).start()

    def sent(parts, where, ok):
        src, dst, send, recv = parts

        @pl.when(both(ok, jnp.logical_not(is_me(where))))
        def _():
            remote(src, dst, send, recv, where).wait_send()

    def landed(parts, where, ok):
        src, dst, send, recv = parts
        here = is_me(where)

        @pl.when(both(ok, jnp.logical_not(here)))
        def _():
            remote(src, dst, send, recv, where).wait_recv()

        @pl.when(both(ok, here))
        def _():
            pltpu.make_async_copy(src, dst, recv).wait()

    def lanes(start, size):
        return pl.ds(pl.multiple_of(start * size, size), size)

    def up_parts(h):
        return q_hbm.at[:, lanes(h, LANE)], qr_ref.at[h], u_send.at[h], u_recv.at[h]

    def up_halo_parts(g):
        return (
            q_hbm.at[CHUNK - 8 : CHUNK, lanes(g, HALFW)], hr_ref.at[g], v_send.at[g], v_recv.at[g]
        )

    def chunk_parts(h, lag):
        return (
            qr_ref.at[h], qg_ref.at[h, lag * EXT + HALO : (lag + 1) * EXT, :],
            q_send.at[h, lag], q_recv.at[h, lag],
        )

    def halo_parts(g, lag):
        return hr_ref.at[g], qh_ref.at[g, lag], h_send.at[g, lag], h_recv.at[g, lag]

    def out_parts(g, lag):
        cols = lanes(g, HALFW)
        return (
            ob_ref.at[lag, :, cols], og_ref.at[lag, :, cols],
            o_send.at[g, lag], o_recv.at[g, lag],
        )

    def stat_parts(g, lag):
        return st_ref.at[g, lag], sg_ref.at[g, lag], s_send.at[g, lag], s_recv.at[g, lag]

    edges = [
        ((k_hbm.at[BLOCK - 16 : BLOCK, :], kn_ref.at[0], n_send.at[0], n_recv.at[0]),
         (qb, kb + 1), kb < 15, (qb, kb - 1), kb > 0),
        ((k_hbm.at[0:16, :], kn_ref.at[1], n_send.at[1], n_recv.at[1]),
         (qb, kb - 1), kb > 0, (qb, kb + 1), kb < 15),
    ]
    for parts, where, ok, _, _ in edges:
        start(parts, where, ok)

    def up_group(g, carry):
        start(up_halo_parts(g), relay(after), halo_out)

        def up_head(p, carry):
            start(up_parts(g * GROUP + p), relay(mine), true)
            return carry

        return lax.fori_loop(0, GROUP, up_head, carry)

    lax.fori_loop(0, GROUPS, up_group, 0)

    load_k.wait()
    for parts, _, _, where, ok in edges:
        landed(parts, where, ok)
    build_edges(k_ref, kn_ref, kt_ref)
    load_v.wait()

    def hand_group(g, carry):
        landed(up_halo_parts(g), owner(held - 1), halo_in)
        for lag in range(SPAN):
            start(halo_parts(g, lag), worker(held, lag), hands[lag])

        def hand_head(p, carry):
            h = g * GROUP + p
            landed(up_parts(h), owner(held), true)
            for lag in range(SPAN):
                start(chunk_parts(h, lag), worker(held, lag), hands[lag])
            return carry

        return lax.fori_loop(0, GROUP, hand_head, carry)

    lax.fori_loop(0, GROUPS, hand_group, 0)

    def arrive(h):
        for lag in range(SPAN):
            landed(chunk_parts(h, lag), relay(chunks[lag]), works[lag])

    def one_group(g, carry):
        for lag in range(SPAN):
            landed(halo_parts(g, lag), relay(chunks[lag]), works[lag])

        def leave(lag):
            where, ok = owner(served(qb, kb, lag)), kb + lag <= 15
            start(stat_parts(g, lag), where, ok)
            start(out_parts(g, lag), where, ok)

        attend_group(
            g, arrive, leave, mw_ref, qg_ref, qh_ref, k_ref, v_ref, kt_ref, w_ref, msc_ref,
            (msk_ref, x_ref, conv_ref, probs_ref, row_ref), ob_ref, st_ref,
        )
        return carry

    lax.fori_loop(0, GROUPS, one_group, 0)

    def one_result(g, carry):
        for lag in range(SPAN):
            landed(stat_parts(g, lag), worker(mine, lag), sends[lag])
            landed(out_parts(g, lag), worker(mine, lag), sends[lag])
        combine_group(g, og_ref, sg_ref, fin_ref, out_ref)
        return carry

    lax.fori_loop(0, GROUPS, one_result, 0)

    for parts, where, ok, _, _ in edges:
        sent(parts, where, ok)

    def drain(g, carry):
        sent(up_halo_parts(g), relay(after), halo_out)
        for lag in range(SPAN):
            sent(halo_parts(g, lag), worker(held, lag), hands[lag])
            sent(stat_parts(g, lag), owner(chunks[lag]), works[lag])
            sent(out_parts(g, lag), owner(chunks[lag]), works[lag])

        def drain_head(p, carry):
            h = g * GROUP + p
            sent(up_parts(h), relay(mine), true)
            for lag in range(SPAN):
                sent(chunk_parts(h, lag), worker(held, lag), hands[lag])
            return carry

        return lax.fori_loop(0, GROUP, drain_head, carry)

    lax.fori_loop(0, GROUPS, drain, 0)


def body(queries, keys, values, conv_weight, mix_weight, doc_ids):
    docs = doc_ids.reshape(-1, LANE)
    taps = conv_weight.transpose(1, 0, 2)
    any_space = pl.BlockSpec(memory_space=pl.ANY)
    vmem = pl.BlockSpec(memory_space=pltpu.VMEM)
    dma = pltpu.SemaphoreType.DMA
    return pl.pallas_call(
        kernel,
        out_shape=jax.ShapeDtypeStruct((CHUNK, WIDTH), BF16),
        in_specs=[
            any_space, any_space, any_space, vmem, pl.BlockSpec(memory_space=pltpu.SMEM), vmem,
        ],
        out_specs=vmem,
        scratch_shapes=[
            pltpu.VMEM((HEADS, EROWS, LANE), BF16),
            pltpu.VMEM((GROUPS, SPAN, 8, HALFW), BF16),
            pltpu.VMEM((BLOCK, WIDTH), BF16),
            pltpu.VMEM((BLOCK, WIDTH), BF16),
            pltpu.VMEM((2, 16, WIDTH), BF16),
            pltpu.VMEM((TILES * LANE, WIDTH), BF16),
            pltpu.VMEM((8 * LAGS, LANE), F32),
            pltpu.VMEM((HEADS, DEPTH, HALF), BF16),
            pltpu.VMEM((2 * TILES, EROWS, LANE), F32),
            pltpu.VMEM((2 * TILES, EROWS, LANE), F32),
            pltpu.VMEM((2 * ROWS, DEPTH), BF16),
            pltpu.VMEM((GROUP, 2 * ROWS, HALF), F32),
            pltpu.VMEM((GROUP, CHUNK, BLOCK), BF16),
            pltpu.VMEM((LANE, LANE), F32),
            pltpu.VMEM((SPAN, CHUNK, WIDTH), BF16),
            pltpu.VMEM((GROUPS, SPAN, 8, LANE), F32),
            pltpu.VMEM((SPAN, CHUNK, WIDTH), BF16),
            pltpu.VMEM((GROUPS, 16, 8, LANE), F32),
            pltpu.VMEM((GROUP, CHUNK, LANE), F32),
            pltpu.VMEM((HEADS, CHUNK, LANE), BF16),
            pltpu.VMEM((GROUPS, 8, HALFW), BF16),
            dma((2,)),
            dma((HEADS, SPAN)), dma((HEADS, SPAN)),
            dma((GROUPS, SPAN)), dma((GROUPS, SPAN)),
            dma((2,)), dma((2,)),
            dma((GROUPS, SPAN)), dma((GROUPS, SPAN)),
            dma((GROUPS, SPAN)), dma((GROUPS, SPAN)),
            dma((HEADS,)), dma((HEADS,)),
            dma((GROUPS,)), dma((GROUPS,)),
        ],
        compiler_params=pltpu.CompilerParams(collective_id=0, has_side_effects=True),
    )(queries, keys, values, taps, mix_weight, docs)


def solution(mesh):
    placed = (
        P(("ba", "qb", "kb"), None),
        P(("ba", "kb"), None),
        P(("ba", "kb"), None),
        P(),
        P(),
        P("ba"),
    )
    return jax.shard_map(
        body, mesh=mesh, in_specs=placed, out_specs=P(("ba", "qb", "kb"), None), check_vma=False
    )
```

```python
import math

import jax
import jax.numpy as jnp
from jax import lax
from jax.experimental import pallas as pl
from jax.experimental.pallas import tpu as pltpu
from jax.sharding import PartitionSpec as P

MESH = pl.DeviceIdType.MESH
F32 = jnp.float32
BF16 = jnp.bfloat16

CHUNK = 64
HALO = 16
EXT = CHUNK + HALO
SPAN = 5
BLOCK = 512
HALF = 256
LANE = 128
LAGS = 6
REACH = 11
SIDE = 5
HEADS = 8
GROUP = 4
GROUPS = 2
TILES = BLOCK // LANE
PAIRS = CHUNK // 2
READS = LAGS + 1
DEPTH = READS * LANE + LANE
ROWS = SPAN * CHUNK
EROWS = SPAN * EXT
HALFW = GROUP * LANE
LOW = -1e30
START = 4
FLIGHT = 2
LOG2E = 1.4426950408889634
WIDTH = HEADS * LANE


def swap(code):
    return code % 2 * 2 + code // 2


def shift(group):
    return swap((group + 2) % 4) + 3 * plane(group)


def plane(group):
    return (group + 14) % 16 // 4


def column(chunk):
    return (chunk % 8 + 64 - shift(chunk // 8)) % 8


def worker(chunk, lag):
    return column(chunk), chunk // 8 - lag


def relay(chunk):
    return column(chunk), plane(chunk // 8) * 4 + chunk % 4


def owner(chunk):
    return chunk // 16, chunk % 16


def served(qb, kb, lag):
    group = kb + lag
    return group * 8 + (qb + shift(group)) % 8


def relayed(qb, kb):
    level = kb // 4
    code = (kb + 64 - qb - 3 * level) % 4
    group = (4 * level + 2 + swap(code)) % 16
    return group * 8 + (qb + code + 3 * level) % 8


def iota(shape, dim):
    return lax.broadcasted_iota(jnp.int32, shape, dim)


def dot_nt(a, b):
    return lax.dot_general(a, b, (((1,), (1,)), ((), ())), preferred_element_type=F32)


def build_masks(qb, kb, doc_ref, msc_ref):
    scale = 1.0 / math.sqrt(LANE)
    docs = doc_ref[...]
    starts = []
    for value in range(1, 8):
        below = (docs < value).astype(F32)
        below = jnp.sum(jnp.sum(below, axis=0, keepdims=True), axis=1, keepdims=True)
        starts.append(jnp.broadcast_to(below.astype(jnp.int32), (EXT, LANE)))
    lane = iota((EXT, LANE), 1)
    first = kb * BLOCK
    edge = lane % 16
    edge = jnp.where(edge < 8, edge - 8, edge + (LANE - 8))
    for lag in range(SPAN):
        row = served(qb, kb, lag) * CHUNK - HALO + iota((EXT, LANE), 0)
        low = jnp.zeros((EXT, LANE), jnp.int32)
        for start in starts:
            low = jnp.where(start <= row, start, low)
        for tile in range(2 * TILES):
            if tile < TILES:
                col = first + tile * LANE + lane
            else:
                col = first + (tile - TILES) * LANE + edge
            good = (col >= low) & (col <= row)
            msc_ref[tile, lag * EXT : (lag + 1) * EXT, :] = jnp.where(good, scale, 0.0).astype(F32)


def build_bands(cw_ref, base_ref, w_ref):
    base_ref[...] = jnp.zeros_like(base_ref)
    center = (iota((HEADS, REACH), 1) == REACH // 2).astype(F32)
    for a in range(LAGS):
        taps = cw_ref[a].astype(F32)
        base_ref[8 * a : 8 * a + HEADS, 0:REACH] = taps + center if a == 0 else taps
    base_ref[...] = pltpu.roll(base_ref[...], LANE - SIDE, 1)
    w_ref[...] = jnp.zeros_like(w_ref)
    diff = iota((LANE, LANE), 1) - iota((LANE, LANE), 0)
    near = (diff <= SIDE) & (diff >= -SIDE)

    def one_head(h, carry):
        for a in range(LAGS):
            ring = jnp.broadcast_to(base_ref[pl.ds(8 * a + h, 1), :], (LANE, LANE))
            ring = pltpu.roll(ring, 0, 1, stride=1, stride_axis=0)
            diag = jnp.where(near, ring, 0.0).astype(BF16)
            upper = jnp.where(diff[LANE - 8 :] <= SIDE - LANE, ring[LANE - 8 :], 0.0)
            lower = jnp.where(diff[:8] >= LANE - SIDE, ring[:8], 0.0)
            rim = jnp.concatenate([upper, lower], axis=0).astype(BF16)
            for e in range(2):
                read = LAGS - 1 - a + e
                edge = READS * LANE + 16 * read
                w_ref[h, read * LANE : (read + 1) * LANE, e * LANE : (e + 1) * LANE] = diag
                w_ref[h, edge : edge + 16, e * LANE : (e + 1) * LANE] = rim
        return carry

    lax.fori_loop(0, HEADS, one_head, 0)


def build_edges(k_ref, kn_ref, kt_ref):
    for t in range(TILES):
        left = k_ref[t * LANE - 16 : t * LANE, :] if t else kn_ref[0]
        right = k_ref[(t + 1) * LANE : (t + 1) * LANE + 16, :] if t < TILES - 1 else kn_ref[1]
        pair = jnp.concatenate([left.astype(F32)[8:16], right.astype(F32)[0:8]], axis=0)
        pair = pair.astype(BF16)
        for a in range(8):
            kt_ref[t * LANE + 16 * a : t * LANE + 16 * a + 16, :] = pair


def attend_group(
    g, arrive, leave, mw_ref, qg_ref, qh_ref, k_ref, v_ref, kt_ref, w_ref, msc_ref, scratch, ob_ref, st_ref
):
    msk_ref, x_ref, conv_ref, probs_ref, row_ref = scratch
    lane = iota((PAIRS, LANE), 1)

    def one_head(p, carry):
        h = g * GROUP + p
        cols = pl.ds(pl.multiple_of(h * LANE, LANE), LANE)
        arrive(h)
        for lag in range(SPAN):
            edge = qh_ref[g, lag, :, pl.ds(pl.multiple_of(p * LANE, LANE), LANE)].astype(F32)
            edge = jnp.concatenate([edge, edge], axis=0).astype(BF16)
            qg_ref[h, lag * EXT : lag * EXT + HALO, :] = edge
        q = qg_ref[h]
        for t in range(TILES):
            part = (t % 2) * HALF
            keys = k_ref[part : part + HALF, cols] if t < 2 else kt_ref[part : part + HALF, cols]
            logits = dot_nt(q, keys)
            for u in range(2):
                msk_ref[2 * t + u] = logits[:, u * LANE : (u + 1) * LANE] * msc_ref[2 * t + u]
        for lag in range(SPAN):
            base = lag * EXT + HALO - (LAGS - 1)
            for t in range(TILES):
                to = (t * SPAN + lag) * PAIRS
                rim = msk_ref[TILES + t, pl.ds(base, PAIRS, stride=2), :]
                for read in range(READS):
                    piece = msk_ref[t, pl.ds(base + read, PAIRS, stride=2), :]
                    x_ref[to : to + PAIRS, read * LANE : (read + 1) * LANE] = piece.astype(BF16)
                    if read:
                        other = msk_ref[TILES + t, pl.ds(base + read, PAIRS, stride=2), :]
                        rim = jnp.where(lane >= 16 * read, other, rim)
                x_ref[to : to + PAIRS, READS * LANE : DEPTH] = rim.astype(BF16)
        conv_ref[p] = jnp.dot(x_ref[...], w_ref[h], preferred_element_type=F32)
        return carry

    lax.fori_loop(0, GROUP, one_head, 0)
    weights = [
        [(mw_ref[g, p, q] + (1.0 if p == q else 0.0)) * LOG2E for q in range(GROUP)] for p in range(GROUP)
    ]
    small = iota((16, LANE), 1)

    def one_lag(lag, carry):
        for b in range(CHUNK // 16):
            parity, half = b // 2, b % 2
            good = [
                msc_ref[tile, pl.ds(lag * EXT + HALO + half * 32 + parity, 16, stride=2), :] > 0
                for tile in range(TILES)
            ]
            conv = [
                [
                    conv_ref[
                        q,
                        pl.ds(pl.multiple_of((tile * SPAN + lag) * PAIRS + half * 16, 16), 16),
                        parity * LANE : (parity + 1) * LANE,
                    ]
                    for tile in range(TILES)
                ]
                for q in range(GROUP)
            ]
            stats = jnp.zeros((16, LANE), F32)
            for p in range(GROUP):
                mixed = []
                for tile in range(4):
                    total = conv[0][tile] * weights[p][0]
                    for q in range(1, GROUP):
                        total = total + conv[q][tile] * weights[p][q]
                    mixed.append(jnp.where(good[tile], total, LOW))
                top = jnp.maximum(
                    jnp.maximum(mixed[0], mixed[1]), jnp.maximum(mixed[2], mixed[3])
                )
                top = jnp.max(top, axis=1, keepdims=True)
                expo = [jnp.exp2(m - top) for m in mixed]
                for tile in range(4):
                    probs_ref[p, b * 16 : b * 16 + 16, tile * LANE : (tile + 1) * LANE] = expo[
                        tile
                    ].astype(BF16)
                total = jnp.sum(
                    (expo[0] + expo[1]) + (expo[2] + expo[3]), axis=1, keepdims=True
                )
                stats = jnp.where(small == p, top, stats)
                stats = jnp.where(small == GROUP + p, total, stats)
            row_ref[b * 16 : b * 16 + 16, :] = stats
        st_ref[g, lag] = row_ref[...].T[0:8, :]
        for p in range(GROUP):
            cols = pl.ds(pl.multiple_of((g * GROUP + p) * LANE, LANE), LANE)
            out = jnp.dot(probs_ref[p], v_ref[:, cols], preferred_element_type=F32)
            ob_ref[lag, :, cols] = out.astype(BF16)
        leave(lag)
        return carry

    lax.fori_loop(0, SPAN, one_lag, 0)


def combine_group(g, og_ref, sg_ref, fin_ref, out_ref):
    tiles = sg_ref[g].reshape(16 * 8, LANE).T[:CHUNK]
    parts = [
        pltpu.roll(tiles, LANE - 8 * lag, 1) if lag else tiles for lag in range(SPAN)
    ]
    top = parts[0]
    for part in parts[1:]:
        top = jnp.maximum(top, part)
    scales = [jnp.exp2(part - top) for part in parts]
    total = jnp.zeros((CHUNK, LANE), F32)
    for part, scale in zip(parts, scales):
        total = total + scale * pltpu.roll(part, LANE - GROUP, 1)
    for p in range(GROUP):
        cols = pl.ds(pl.multiple_of((g * GROUP + p) * LANE, LANE), LANE)
        acc = jnp.zeros((CHUNK, LANE), F32)
        for lag in range(SPAN):
            acc = acc + og_ref[lag, :, cols].astype(F32) * scales[lag][:, p : p + 1]
        acc = acc / total[:, p : p + 1]
        for parity in range(2):
            fin_ref[p, pl.ds(parity, PAIRS, stride=2), :] = acc[
                parity * PAIRS : (parity + 1) * PAIRS
            ]
        out_ref[:, cols] = fin_ref[p].astype(BF16)


def kernel(
    q_hbm, k_hbm, v_hbm, cw_ref, mw_ref, doc_ref, out_ref,
    qg_ref, qh_ref, k_ref, v_ref, kn_ref, kt_ref, base_ref, w_ref, msc_ref,
    msk_ref, x_ref, conv_ref, probs_ref, row_ref, ob_ref, st_ref, og_ref, sg_ref, fin_ref, qr_ref, hr_ref,
    local_sem, q_send, q_recv, h_send, h_recv, n_send, n_recv, o_send, o_recv, s_send, s_recv,
    u_send, u_recv, v_send, v_recv,
):
    qb, kb = lax.axis_index("qb"), lax.axis_index("kb")
    mine = qb * 16 + kb
    after = mine + 1
    held = relayed(qb, kb)
    chunks = [served(qb, kb, lag) for lag in range(SPAN)]

    def is_me(where):
        return jnp.logical_and(where[0] == qb, where[1] == kb)

    def both(a, b):
        return jnp.logical_and(a, b)

    def place(where):
        return {"qb": where[0], "kb": where[1]}

    true = kb >= 0
    works = [kb + lag <= 15 for lag in range(SPAN)]
    sends = [mine // 8 >= lag for lag in range(SPAN)]
    hands = [held // 8 >= lag for lag in range(SPAN)]
    last = mine == 127
    first = held == 0
    halo_out, halo_in = jnp.logical_not(last), jnp.logical_not(first)

    barrier = pltpu.get_barrier_semaphore()

    def greet(where, ok):
        @pl.when(both(ok, jnp.logical_not(is_me(where))))
        def _():
            pl.semaphore_signal(barrier, inc=1, device_id=place(where), device_id_type=MESH)

    greet((qb, kb + 1), kb < 15)
    greet((qb, kb - 1), kb > 0)
    greet(owner(held), true)
    greet(owner(held - 1), halo_in)
    for lag in range(SPAN):
        greet(relay(chunks[lag]), works[lag])
    senders = [
        ((qb, kb + 1), kb < 15), ((qb, kb - 1), kb > 0),
        (relay(mine), true), (relay(after), halo_out),
    ]
    senders += [(worker(held, lag), hands[lag]) for lag in range(SPAN)]
    count = jnp.int32(0)
    for where, ok in senders:
        count = count + both(ok, jnp.logical_not(is_me(where))).astype(jnp.int32)

    load_k = pltpu.make_async_copy(k_hbm, k_ref, local_sem.at[0])
    load_v = pltpu.make_async_copy(v_hbm, v_ref, local_sem.at[1])
    load_k.start()
    load_v.start()

    @pl.when(kb == 0)
    def _():
        kn_ref[0] = jnp.zeros((16, WIDTH), BF16)

    @pl.when(kb == 15)
    def _():
        kn_ref[1] = jnp.zeros((16, WIDTH), BF16)

    @pl.when(first)
    def _():
        hr_ref[...] = jnp.zeros_like(hr_ref)

    for lag in range(1, SPAN):
        @pl.when(jnp.logical_not(sends[lag]))
        def _():
            og_ref[lag] = jnp.zeros((CHUNK, WIDTH), BF16)
    sg_ref[...] = jnp.full(sg_ref.shape, LOW, F32)

    build_masks(qb, kb, doc_ref, msc_ref)
    build_bands(cw_ref, base_ref, w_ref)
    pl.semaphore_wait(barrier, count)

    def remote(src, dst, send, recv, where):
        return pltpu.make_async_remote_copy(
            src_ref=src, dst_ref=dst, send_sem=send, recv_sem=recv,
            device_id=place(where), device_id_type=MESH,
        )

    def start(parts, where, ok):
        src, dst, send, recv = parts
        here = is_me(where)

        @pl.when(both(ok, jnp.logical_not(here)))
        def _():
            remote(src, dst, send, recv, where).start()

        @pl.when(both(ok, here))
        def _():
            pltpu.make_async_copy(src, dst, recv).start()

    def sent(parts, where, ok):
        src, dst, send, recv = parts

        @pl.when(both(ok, jnp.logical_not(is_me(where))))
        def _():
            remote(src, dst, send, recv, where).wait_send()

    def landed(parts, where, ok):
        src, dst, send, recv = parts
        here = is_me(where)

        @pl.when(both(ok, jnp.logical_not(here)))
        def _():
            remote(src, dst, send, recv, where).wait_recv()

        @pl.when(both(ok, here))
        def _():
            pltpu.make_async_copy(src, dst, recv).wait()

    def lanes(start, size):
        return pl.ds(pl.multiple_of(start * size, size), size)

    def up_parts(h):
        return q_hbm.at[:, lanes(h, LANE)], qr_ref.at[h], u_send.at[h], u_recv.at[h]

    def up_halo_parts(g):
        return (
            q_hbm.at[CHUNK - 8 : CHUNK, lanes(g, HALFW)], hr_ref.at[g], v_send.at[g], v_recv.at[g]
        )

    def chunk_parts(h, lag):
        return (
            qr_ref.at[h], qg_ref.at[h, lag * EXT + HALO : (lag + 1) * EXT, :],
            q_send.at[h, lag], q_recv.at[h, lag],
        )

    def halo_parts(g, lag):
        return hr_ref.at[g], qh_ref.at[g, lag], h_send.at[g, lag], h_recv.at[g, lag]

    def out_parts(g, lag):
        cols = lanes(g, HALFW)
        return (
            ob_ref.at[lag, :, cols], og_ref.at[lag, :, cols],
            o_send.at[g, lag], o_recv.at[g, lag],
        )

    def stat_parts(g, lag):
        return st_ref.at[g, lag], sg_ref.at[g, lag], s_send.at[g, lag], s_recv.at[g, lag]

    edges = [
        ((k_hbm.at[BLOCK - 16 : BLOCK, :], kn_ref.at[0], n_send.at[0], n_recv.at[0]),
         (qb, kb + 1), kb < 15, (qb, kb - 1), kb > 0),
        ((k_hbm.at[0:16, :], kn_ref.at[1], n_send.at[1], n_recv.at[1]),
         (qb, kb - 1), kb > 0, (qb, kb + 1), kb < 15),
    ]
    for parts, where, ok, _, _ in edges:
        start(parts, where, ok)

    def up_group(g, carry):
        start(up_halo_parts(g), relay(after), halo_out)

        def up_head(p, carry):
            start(up_parts(g * GROUP + p), relay(mine), true)
            return carry

        return lax.fori_loop(0, GROUP, up_head, carry)

    lax.fori_loop(0, GROUPS, up_group, 0)

    load_k.wait()
    for parts, _, _, where, ok in edges:
        landed(parts, where, ok)
    build_edges(k_ref, kn_ref, kt_ref)
    load_v.wait()

    def hand(h, carry):
        @pl.when(jnp.logical_and(h >= FLIGHT, h < START))
        def _():
            for lag in range(SPAN):
                sent(chunk_parts(h - FLIGHT, lag), worker(held, lag), hands[lag])

        @pl.when(h % GROUP == 0)
        def _():
            g = h // GROUP
            landed(up_halo_parts(g), owner(held - 1), halo_in)
            for lag in range(SPAN):
                start(halo_parts(g, lag), worker(held, lag), hands[lag])

        landed(up_parts(h), owner(held), true)
        for lag in range(SPAN):
            start(chunk_parts(h, lag), worker(held, lag), hands[lag])
        return carry

    lax.fori_loop(0, START, hand, 0)

    def arrive(h):
        @pl.when(h + START < HEADS)
        def _():
            hand(h + START, 0)

        for lag in range(SPAN):
            landed(chunk_parts(h, lag), relay(chunks[lag]), works[lag])

    def one_group(g, carry):
        for lag in range(SPAN):
            landed(halo_parts(g, lag), relay(chunks[lag]), works[lag])

        def leave(lag):
            where, ok = owner(served(qb, kb, lag)), kb + lag <= 15
            start(stat_parts(g, lag), where, ok)
            start(out_parts(g, lag), where, ok)

        attend_group(
            g, arrive, leave, mw_ref, qg_ref, qh_ref, k_ref, v_ref, kt_ref, w_ref, msc_ref,
            (msk_ref, x_ref, conv_ref, probs_ref, row_ref), ob_ref, st_ref,
        )
        return carry

    lax.fori_loop(0, GROUPS, one_group, 0)

    def drain_head(h, carry):
        sent(up_parts(h), relay(mine), true)

        @pl.when(h >= START - FLIGHT)
        def _():
            for lag in range(SPAN):
                sent(chunk_parts(h, lag), worker(held, lag), hands[lag])

        return carry

    def drain_halo(g, carry):
        sent(up_halo_parts(g), relay(after), halo_out)
        for lag in range(SPAN):
            sent(halo_parts(g, lag), worker(held, lag), hands[lag])
        return carry

    def one_result(g, carry):
        @pl.when(g == 1)
        def _():
            for parts, where, ok, _, _ in edges:
                sent(parts, where, ok)
            lax.fori_loop(0, HEADS, drain_head, 0)
            lax.fori_loop(0, GROUPS, drain_halo, 0)

        for lag in range(SPAN):
            landed(stat_parts(g, lag), worker(mine, lag), sends[lag])
            landed(out_parts(g, lag), worker(mine, lag), sends[lag])
        combine_group(g, og_ref, sg_ref, fin_ref, out_ref)
        return carry

    lax.fori_loop(0, GROUPS, one_result, 0)

    def drain_out(g, carry):
        for lag in range(SPAN):
            sent(stat_parts(g, lag), owner(chunks[lag]), works[lag])
            sent(out_parts(g, lag), owner(chunks[lag]), works[lag])
        return carry

    lax.fori_loop(0, GROUPS, drain_out, 0)


def body(queries, keys, values, conv_weight, mix_weight, doc_ids):
    docs = doc_ids.reshape(-1, LANE)
    taps = conv_weight.transpose(1, 0, 2)
    any_space = pl.BlockSpec(memory_space=pl.ANY)
    vmem = pl.BlockSpec(memory_space=pltpu.VMEM)
    dma = pltpu.SemaphoreType.DMA
    return pl.pallas_call(
        kernel,
        out_shape=jax.ShapeDtypeStruct((CHUNK, WIDTH), BF16),
        in_specs=[
            any_space, any_space, any_space, vmem, pl.BlockSpec(memory_space=pltpu.SMEM), vmem,
        ],
        out_specs=vmem,
        scratch_shapes=[
            pltpu.VMEM((HEADS, EROWS, LANE), BF16),
            pltpu.VMEM((GROUPS, SPAN, 8, HALFW), BF16),
            pltpu.VMEM((BLOCK, WIDTH), BF16),
            pltpu.VMEM((BLOCK, WIDTH), BF16),
            pltpu.VMEM((2, 16, WIDTH), BF16),
            pltpu.VMEM((TILES * LANE, WIDTH), BF16),
            pltpu.VMEM((8 * LAGS, LANE), F32),
            pltpu.VMEM((HEADS, DEPTH, HALF), BF16),
            pltpu.VMEM((2 * TILES, EROWS, LANE), F32),
            pltpu.VMEM((2 * TILES, EROWS, LANE), F32),
            pltpu.VMEM((2 * ROWS, DEPTH), BF16),
            pltpu.VMEM((GROUP, 2 * ROWS, HALF), F32),
            pltpu.VMEM((GROUP, CHUNK, BLOCK), BF16),
            pltpu.VMEM((LANE, LANE), F32),
            pltpu.VMEM((SPAN, CHUNK, WIDTH), BF16),
            pltpu.VMEM((GROUPS, SPAN, 8, LANE), F32),
            pltpu.VMEM((SPAN, CHUNK, WIDTH), BF16),
            pltpu.VMEM((GROUPS, 16, 8, LANE), F32),
            pltpu.VMEM((GROUP, CHUNK, LANE), F32),
            pltpu.VMEM((HEADS, CHUNK, LANE), BF16),
            pltpu.VMEM((GROUPS, 8, HALFW), BF16),
            dma((2,)),
            dma((HEADS, SPAN)), dma((HEADS, SPAN)),
            dma((GROUPS, SPAN)), dma((GROUPS, SPAN)),
            dma((2,)), dma((2,)),
            dma((GROUPS, SPAN)), dma((GROUPS, SPAN)),
            dma((GROUPS, SPAN)), dma((GROUPS, SPAN)),
            dma((HEADS,)), dma((HEADS,)),
            dma((GROUPS,)), dma((GROUPS,)),
        ],
        compiler_params=pltpu.CompilerParams(collective_id=0, has_side_effects=True),
    )(queries, keys, values, taps, mix_weight, docs)


def solution(mesh):
    placed = (
        P(("ba", "qb", "kb"), None),
        P(("ba", "kb"), None),
        P(("ba", "kb"), None),
        P(),
        P(),
        P("ba"),
    )
    return jax.shard_map(
        body, mesh=mesh, in_specs=placed, out_specs=P(("ba", "qb", "kb"), None), check_vma=False
    )
```

```python
import math

import jax
import jax.numpy as jnp
from jax import lax
from jax.experimental import pallas as pl
from jax.experimental.pallas import tpu as pltpu
from jax.sharding import PartitionSpec as P

MESH = pl.DeviceIdType.MESH
F32 = jnp.float32
BF16 = jnp.bfloat16

CHUNK = 64
HALO = 16
EXT = CHUNK + HALO
SPAN = 5
BLOCK = 512
HALF = 256
LANE = 128
LAGS = 6
REACH = 11
SIDE = 5
HEADS = 8
GROUP = 4
GROUPS = 2
TILES = BLOCK // LANE
PAIRS = CHUNK // 2
READS = LAGS + 1
DEPTH = READS * LANE + LANE
ROWS = SPAN * CHUNK
EROWS = SPAN * EXT
HALFW = GROUP * LANE
LOW = -1e30
START = 4
FLIGHT = 2
LOG2E = 1.4426950408889634
WIDTH = HEADS * LANE


def swap(code):
    return code % 2 * 2 + code // 2


def shift(group):
    return swap((group + 2) % 4) + 3 * plane(group)


def plane(group):
    return (group + 14) % 16 // 4


def column(chunk):
    return (chunk % 8 + 64 - shift(chunk // 8)) % 8


def worker(chunk, lag):
    return column(chunk), chunk // 8 - lag


def relay(chunk):
    return column(chunk), plane(chunk // 8) * 4 + chunk % 4


def owner(chunk):
    return chunk // 16, chunk % 16


def served(qb, kb, lag):
    group = kb + lag
    return group * 8 + (qb + shift(group)) % 8


def relayed(qb, kb):
    level = kb // 4
    code = (kb + 64 - qb - 3 * level) % 4
    group = (4 * level + 2 + swap(code)) % 16
    return group * 8 + (qb + code + 3 * level) % 8


def iota(shape, dim):
    return lax.broadcasted_iota(jnp.int32, shape, dim)


def dot_nt(a, b):
    return lax.dot_general(a, b, (((1,), (1,)), ((), ())), preferred_element_type=F32)


def build_masks(qb, kb, doc_ref, msc_ref):
    scale = 1.0 / math.sqrt(LANE)
    docs = doc_ref[...]
    starts = []
    for value in range(1, 8):
        below = (docs < value).astype(F32)
        below = jnp.sum(jnp.sum(below, axis=0, keepdims=True), axis=1, keepdims=True)
        starts.append(jnp.broadcast_to(below.astype(jnp.int32), (EXT, LANE)))
    lane = iota((EXT, LANE), 1)
    first = kb * BLOCK
    edge = lane % 16
    edge = jnp.where(edge < 8, edge - 8, edge + (LANE - 8))
    for lag in range(SPAN):
        row = served(qb, kb, lag) * CHUNK - HALO + iota((EXT, LANE), 0)
        low = jnp.zeros((EXT, LANE), jnp.int32)
        for start in starts:
            low = jnp.where(start <= row, start, low)
        for tile in range(2 * TILES):
            if tile < TILES:
                col = first + tile * LANE + lane
            else:
                col = first + (tile - TILES) * LANE + edge
            good = (col >= low) & (col <= row)
            msc_ref[tile, lag * EXT : (lag + 1) * EXT, :] = jnp.where(good, scale, 0.0).astype(F32)


def build_bands(cw_ref, base_ref, w_ref):
    base_ref[...] = jnp.zeros_like(base_ref)
    center = (iota((HEADS, REACH), 1) == REACH // 2).astype(F32)
    for a in range(LAGS):
        taps = cw_ref[a].astype(F32)
        base_ref[8 * a : 8 * a + HEADS, 0:REACH] = taps + center if a == 0 else taps
    base_ref[...] = pltpu.roll(base_ref[...], LANE - SIDE, 1)
    w_ref[...] = jnp.zeros_like(w_ref)
    diff = iota((LANE, LANE), 1) - iota((LANE, LANE), 0)
    near = (diff <= SIDE) & (diff >= -SIDE)

    def one_head(h, carry):
        for a in range(LAGS):
            ring = jnp.broadcast_to(base_ref[pl.ds(8 * a + h, 1), :], (LANE, LANE))
            ring = pltpu.roll(ring, 0, 1, stride=1, stride_axis=0)
            diag = jnp.where(near, ring, 0.0).astype(BF16)
            upper = jnp.where(diff[LANE - 8 :] <= SIDE - LANE, ring[LANE - 8 :], 0.0)
            lower = jnp.where(diff[:8] >= LANE - SIDE, ring[:8], 0.0)
            rim = jnp.concatenate([upper, lower], axis=0).astype(BF16)
            for e in range(2):
                read = LAGS - 1 - a + e
                edge = READS * LANE + 16 * read
                w_ref[h, read * LANE : (read + 1) * LANE, e * LANE : (e + 1) * LANE] = diag
                w_ref[h, edge : edge + 16, e * LANE : (e + 1) * LANE] = rim
        return carry

    lax.fori_loop(0, HEADS, one_head, 0)


def build_edges(k_ref, kn_ref, kt_ref):
    for t in range(TILES):
        left = k_ref[t * LANE - 16 : t * LANE, :] if t else kn_ref[0]
        right = k_ref[(t + 1) * LANE : (t + 1) * LANE + 16, :] if t < TILES - 1 else kn_ref[1]
        pair = jnp.concatenate([left.astype(F32)[8:16], right.astype(F32)[0:8]], axis=0)
        pair = pair.astype(BF16)
        for a in range(8):
            kt_ref[t * LANE + 16 * a : t * LANE + 16 * a + 16, :] = pair


def attend_group(
    g, arrive, leave, mw_ref, qg_ref, qh_ref, k_ref, v_ref, kt_ref, w_ref, msc_ref, scratch, ob_ref, st_ref
):
    msk_ref, x_ref, conv_ref, probs_ref, row_ref = scratch
    lane = iota((PAIRS, LANE), 1)

    def one_head(p, carry):
        h = g * GROUP + p
        cols = pl.ds(pl.multiple_of(h * LANE, LANE), LANE)
        arrive(h)
        for lag in range(SPAN):
            edge = qh_ref[g, lag, :, pl.ds(pl.multiple_of(p * LANE, LANE), LANE)].astype(F32)
            edge = jnp.concatenate([edge, edge], axis=0).astype(BF16)
            qg_ref[h, lag * EXT : lag * EXT + HALO, :] = edge
        q = qg_ref[h]
        for t in range(TILES):
            part = (t % 2) * HALF
            keys = k_ref[part : part + HALF, cols] if t < 2 else kt_ref[part : part + HALF, cols]
            logits = dot_nt(q, keys)
            for u in range(2):
                msk_ref[2 * t + u] = logits[:, u * LANE : (u + 1) * LANE] * msc_ref[2 * t + u]
        for lag in range(SPAN):
            base = lag * EXT + HALO - (LAGS - 1)
            for t in range(TILES):
                to = (t * SPAN + lag) * PAIRS
                rim = msk_ref[TILES + t, pl.ds(base, PAIRS, stride=2), :]
                for read in range(READS):
                    piece = msk_ref[t, pl.ds(base + read, PAIRS, stride=2), :]
                    x_ref[to : to + PAIRS, read * LANE : (read + 1) * LANE] = piece.astype(BF16)
                    if read:
                        other = msk_ref[TILES + t, pl.ds(base + read, PAIRS, stride=2), :]
                        rim = jnp.where(lane >= 16 * read, other, rim)
                x_ref[to : to + PAIRS, READS * LANE : DEPTH] = rim.astype(BF16)
        conv_ref[p] = jnp.dot(x_ref[...], w_ref[h], preferred_element_type=F32)
        return carry

    lax.fori_loop(0, GROUP, one_head, 0)
    weights = [
        [(mw_ref[g, p, q] + (1.0 if p == q else 0.0)) * LOG2E for q in range(GROUP)] for p in range(GROUP)
    ]
    small = iota((16, LANE), 1)

    def one_lag(lag, carry):
        for b in range(CHUNK // 16):
            parity, half = b // 2, b % 2
            good = [
                msc_ref[tile, pl.ds(lag * EXT + HALO + half * 32 + parity, 16, stride=2), :] > 0
                for tile in range(TILES)
            ]
            conv = [
                [
                    conv_ref[
                        q,
                        pl.ds(pl.multiple_of((tile * SPAN + lag) * PAIRS + half * 16, 16), 16),
                        parity * LANE : (parity + 1) * LANE,
                    ]
                    for tile in range(TILES)
                ]
                for q in range(GROUP)
            ]
            stats = jnp.zeros((16, LANE), F32)
            for p in range(GROUP):
                mixed = []
                for tile in range(4):
                    total = conv[0][tile] * weights[p][0]
                    for q in range(1, GROUP):
                        total = total + conv[q][tile] * weights[p][q]
                    mixed.append(jnp.where(good[tile], total, LOW))
                top = jnp.maximum(
                    jnp.maximum(mixed[0], mixed[1]), jnp.maximum(mixed[2], mixed[3])
                )
                top = jnp.max(top, axis=1, keepdims=True)
                expo = [jnp.exp2(m - top) for m in mixed]
                for tile in range(4):
                    probs_ref[p, b * 16 : b * 16 + 16, tile * LANE : (tile + 1) * LANE] = expo[
                        tile
                    ].astype(BF16)
                total = jnp.sum(
                    (expo[0] + expo[1]) + (expo[2] + expo[3]), axis=1, keepdims=True
                )
                stats = jnp.where(small == p, top, stats)
                stats = jnp.where(small == GROUP + p, total, stats)
            row_ref[b * 16 : b * 16 + 16, :] = stats
        st_ref[g, lag] = row_ref[...].T[0:8, :]
        for p in range(GROUP):
            cols = pl.ds(pl.multiple_of((g * GROUP + p) * LANE, LANE), LANE)
            out = jnp.dot(probs_ref[p], v_ref[:, cols], preferred_element_type=F32)
            ob_ref[lag, :, cols] = out.astype(BF16)
        leave(lag)
        return carry

    lax.fori_loop(0, SPAN, one_lag, 0)


def combine_group(g, og_ref, sg_ref, fin_ref, out_ref):
    tiles = sg_ref[g].reshape(16 * 8, LANE).T[:CHUNK]
    parts = [
        pltpu.roll(tiles, LANE - 8 * lag, 1) if lag else tiles for lag in range(SPAN)
    ]
    top = parts[0]
    for part in parts[1:]:
        top = jnp.maximum(top, part)
    scales = [jnp.exp2(part - top) for part in parts]
    total = jnp.zeros((CHUNK, LANE), F32)
    for part, scale in zip(parts, scales):
        total = total + scale * pltpu.roll(part, LANE - GROUP, 1)
    for p in range(GROUP):
        cols = pl.ds(pl.multiple_of((g * GROUP + p) * LANE, LANE), LANE)
        acc = jnp.zeros((CHUNK, LANE), F32)
        for lag in range(SPAN):
            acc = acc + og_ref[lag, :, cols].astype(F32) * scales[lag][:, p : p + 1]
        acc = acc / total[:, p : p + 1]
        for parity in range(2):
            fin_ref[p, pl.ds(parity, PAIRS, stride=2), :] = acc[
                parity * PAIRS : (parity + 1) * PAIRS
            ]
        out_ref[:, cols] = fin_ref[p].astype(BF16)


def kernel(
    q_hbm, k_hbm, v_hbm, cw_ref, mw_ref, doc_ref, out_ref,
    qg_ref, qh_ref, k_ref, v_ref, kn_ref, kt_ref, base_ref, w_ref, msc_ref,
    msk_ref, x_ref, conv_ref, probs_ref, row_ref, ob_ref, st_ref, og_ref, sg_ref, fin_ref, qr_ref, hr_ref,
    local_sem, q_send, q_recv, h_send, h_recv, n_send, n_recv, o_send, o_recv, s_send, s_recv,
    u_send, u_recv, v_send, v_recv,
):
    qb, kb = lax.axis_index("qb"), lax.axis_index("kb")
    mine = qb * 16 + kb
    after = mine + 1
    held = relayed(qb, kb)
    chunks = [served(qb, kb, lag) for lag in range(SPAN)]

    def is_me(where):
        return jnp.logical_and(where[0] == qb, where[1] == kb)

    def both(a, b):
        return jnp.logical_and(a, b)

    def place(where):
        return {"qb": where[0], "kb": where[1]}

    true = kb >= 0
    works = [kb + lag <= 15 for lag in range(SPAN)]
    sends = [mine // 8 >= lag for lag in range(SPAN)]
    hands = [held // 8 >= lag for lag in range(SPAN)]
    last = mine == 127
    first = held == 0
    halo_out, halo_in = jnp.logical_not(last), jnp.logical_not(first)

    barrier = pltpu.get_barrier_semaphore()

    def greet(where, ok):
        @pl.when(both(ok, jnp.logical_not(is_me(where))))
        def _():
            pl.semaphore_signal(barrier, inc=1, device_id=place(where), device_id_type=MESH)

    greet((qb, kb + 1), kb < 15)
    greet((qb, kb - 1), kb > 0)
    greet(owner(held), true)
    greet(owner(held - 1), halo_in)
    for lag in range(SPAN):
        greet(relay(chunks[lag]), works[lag])
    senders = [
        ((qb, kb + 1), kb < 15), ((qb, kb - 1), kb > 0),
        (relay(mine), true), (relay(after), halo_out),
    ]
    senders += [(worker(held, lag), hands[lag]) for lag in range(SPAN)]
    count = jnp.int32(0)
    for where, ok in senders:
        count = count + both(ok, jnp.logical_not(is_me(where))).astype(jnp.int32)

    load_k = pltpu.make_async_copy(k_hbm, k_ref, local_sem.at[0])
    load_v = pltpu.make_async_copy(v_hbm, v_ref, local_sem.at[1])
    load_k.start()
    load_v.start()

    @pl.when(kb == 0)
    def _():
        kn_ref[0] = jnp.zeros((16, WIDTH), BF16)

    @pl.when(kb == 15)
    def _():
        kn_ref[1] = jnp.zeros((16, WIDTH), BF16)

    @pl.when(first)
    def _():
        hr_ref[...] = jnp.zeros_like(hr_ref)

    for lag in range(1, SPAN):
        @pl.when(jnp.logical_not(sends[lag]))
        def _():
            og_ref[lag] = jnp.zeros((CHUNK, WIDTH), BF16)
    sg_ref[...] = jnp.full(sg_ref.shape, LOW, F32)

    build_masks(qb, kb, doc_ref, msc_ref)
    build_bands(cw_ref, base_ref, w_ref)
    pl.semaphore_wait(barrier, count)

    def remote(src, dst, send, recv, where):
        return pltpu.make_async_remote_copy(
            src_ref=src, dst_ref=dst, send_sem=send, recv_sem=recv,
            device_id=place(where), device_id_type=MESH,
        )

    def start(parts, where, ok):
        src, dst, send, recv = parts
        here = is_me(where)

        @pl.when(both(ok, jnp.logical_not(here)))
        def _():
            remote(src, dst, send, recv, where).start()

        @pl.when(both(ok, here))
        def _():
            pltpu.make_async_copy(src, dst, recv).start()

    def sent(parts, where, ok):
        src, dst, send, recv = parts

        @pl.when(both(ok, jnp.logical_not(is_me(where))))
        def _():
            remote(src, dst, send, recv, where).wait_send()

    def landed(parts, where, ok):
        src, dst, send, recv = parts
        here = is_me(where)

        @pl.when(both(ok, jnp.logical_not(here)))
        def _():
            remote(src, dst, send, recv, where).wait_recv()

        @pl.when(both(ok, here))
        def _():
            pltpu.make_async_copy(src, dst, recv).wait()

    def lanes(start, size):
        return pl.ds(pl.multiple_of(start * size, size), size)

    def up_parts(h):
        return q_hbm.at[:, lanes(h, LANE)], qr_ref.at[h], u_send.at[h], u_recv.at[h]

    def up_halo_parts(g):
        return (
            q_hbm.at[CHUNK - 8 : CHUNK, lanes(g, HALFW)], hr_ref.at[g], v_send.at[g], v_recv.at[g]
        )

    def chunk_parts(h, lag):
        return (
            qr_ref.at[h], qg_ref.at[h, lag * EXT + HALO : (lag + 1) * EXT, :],
            q_send.at[h, lag], q_recv.at[h, lag],
        )

    def halo_parts(g, lag):
        return hr_ref.at[g], qh_ref.at[g, lag], h_send.at[g, lag], h_recv.at[g, lag]

    def out_parts(g, lag):
        cols = lanes(g, HALFW)
        return (
            ob_ref.at[lag, :, cols], og_ref.at[lag, :, cols],
            o_send.at[g, lag], o_recv.at[g, lag],
        )

    def stat_parts(g, lag):
        return st_ref.at[g, lag], sg_ref.at[g, lag], s_send.at[g, lag], s_recv.at[g, lag]

    edges = [
        ((k_hbm.at[BLOCK - 16 : BLOCK, :], kn_ref.at[0], n_send.at[0], n_recv.at[0]),
         (qb, kb + 1), kb < 15, (qb, kb - 1), kb > 0),
        ((k_hbm.at[0:16, :], kn_ref.at[1], n_send.at[1], n_recv.at[1]),
         (qb, kb - 1), kb > 0, (qb, kb + 1), kb < 15),
    ]
    for parts, where, ok, _, _ in edges:
        start(parts, where, ok)

    def up_group(g, carry):
        start(up_halo_parts(g), relay(after), halo_out)

        def up_head(p, carry):
            start(up_parts(g * GROUP + p), relay(mine), true)
            return carry

        return lax.fori_loop(0, GROUP, up_head, carry)

    lax.fori_loop(0, GROUPS, up_group, 0)

    load_k.wait()
    for parts, _, _, where, ok in edges:
        landed(parts, where, ok)
    build_edges(k_ref, kn_ref, kt_ref)
    load_v.wait()

    def hand(h, carry):
        @pl.when(jnp.logical_and(h >= FLIGHT, h < START))
        def _():
            for lag in range(SPAN):
                sent(chunk_parts(h - FLIGHT, lag), worker(held, lag), hands[lag])

        @pl.when(h % GROUP == 0)
        def _():
            g = h // GROUP
            landed(up_halo_parts(g), owner(held - 1), halo_in)
            for lag in range(SPAN):
                start(halo_parts(g, lag), worker(held, lag), hands[lag])

        landed(up_parts(h), owner(held), true)
        for lag in reversed(range(SPAN)):
            start(chunk_parts(h, lag), worker(held, lag), hands[lag])
        return carry

    lax.fori_loop(0, START, hand, 0)

    def arrive(h):
        @pl.when(h + START < HEADS)
        def _():
            hand(h + START, 0)

        for lag in range(SPAN):
            landed(chunk_parts(h, lag), relay(chunks[lag]), works[lag])

    def one_group(g, carry):
        for lag in range(SPAN):
            landed(halo_parts(g, lag), relay(chunks[lag]), works[lag])

        def leave(lag):
            where, ok = owner(served(qb, kb, lag)), kb + lag <= 15
            start(stat_parts(g, lag), where, ok)
            start(out_parts(g, lag), where, ok)

        attend_group(
            g, arrive, leave, mw_ref, qg_ref, qh_ref, k_ref, v_ref, kt_ref, w_ref, msc_ref,
            (msk_ref, x_ref, conv_ref, probs_ref, row_ref), ob_ref, st_ref,
        )
        return carry

    lax.fori_loop(0, GROUPS, one_group, 0)

    def drain_head(h, carry):
        sent(up_parts(h), relay(mine), true)

        @pl.when(h >= START - FLIGHT)
        def _():
            for lag in range(SPAN):
                sent(chunk_parts(h, lag), worker(held, lag), hands[lag])

        return carry

    def drain_halo(g, carry):
        sent(up_halo_parts(g), relay(after), halo_out)
        for lag in range(SPAN):
            sent(halo_parts(g, lag), worker(held, lag), hands[lag])
        return carry

    def one_result(g, carry):
        @pl.when(g == 1)
        def _():
            for parts, where, ok, _, _ in edges:
                sent(parts, where, ok)
            lax.fori_loop(0, HEADS, drain_head, 0)
            lax.fori_loop(0, GROUPS, drain_halo, 0)

        for lag in range(SPAN):
            landed(stat_parts(g, lag), worker(mine, lag), sends[lag])
            landed(out_parts(g, lag), worker(mine, lag), sends[lag])
        combine_group(g, og_ref, sg_ref, fin_ref, out_ref)
        return carry

    lax.fori_loop(0, GROUPS, one_result, 0)

    def drain_out(g, carry):
        for lag in range(SPAN):
            sent(stat_parts(g, lag), owner(chunks[lag]), works[lag])
            sent(out_parts(g, lag), owner(chunks[lag]), works[lag])
        return carry

    lax.fori_loop(0, GROUPS, drain_out, 0)


def body(queries, keys, values, conv_weight, mix_weight, doc_ids):
    docs = doc_ids.reshape(-1, LANE)
    taps = conv_weight.transpose(1, 0, 2)
    any_space = pl.BlockSpec(memory_space=pl.ANY)
    vmem = pl.BlockSpec(memory_space=pltpu.VMEM)
    dma = pltpu.SemaphoreType.DMA
    return pl.pallas_call(
        kernel,
        out_shape=jax.ShapeDtypeStruct((CHUNK, WIDTH), BF16),
        in_specs=[
            any_space, any_space, any_space, vmem, pl.BlockSpec(memory_space=pltpu.SMEM), vmem,
        ],
        out_specs=vmem,
        scratch_shapes=[
            pltpu.VMEM((HEADS, EROWS, LANE), BF16),
            pltpu.VMEM((GROUPS, SPAN, 8, HALFW), BF16),
            pltpu.VMEM((BLOCK, WIDTH), BF16),
            pltpu.VMEM((BLOCK, WIDTH), BF16),
            pltpu.VMEM((2, 16, WIDTH), BF16),
            pltpu.VMEM((TILES * LANE, WIDTH), BF16),
            pltpu.VMEM((8 * LAGS, LANE), F32),
            pltpu.VMEM((HEADS, DEPTH, HALF), BF16),
            pltpu.VMEM((2 * TILES, EROWS, LANE), F32),
            pltpu.VMEM((2 * TILES, EROWS, LANE), F32),
            pltpu.VMEM((2 * ROWS, DEPTH), BF16),
            pltpu.VMEM((GROUP, 2 * ROWS, HALF), F32),
            pltpu.VMEM((GROUP, CHUNK, BLOCK), BF16),
            pltpu.VMEM((LANE, LANE), F32),
            pltpu.VMEM((SPAN, CHUNK, WIDTH), BF16),
            pltpu.VMEM((GROUPS, SPAN, 8, LANE), F32),
            pltpu.VMEM((SPAN, CHUNK, WIDTH), BF16),
            pltpu.VMEM((GROUPS, 16, 8, LANE), F32),
            pltpu.VMEM((GROUP, CHUNK, LANE), F32),
            pltpu.VMEM((HEADS, CHUNK, LANE), BF16),
            pltpu.VMEM((GROUPS, 8, HALFW), BF16),
            dma((2,)),
            dma((HEADS, SPAN)), dma((HEADS, SPAN)),
            dma((GROUPS, SPAN)), dma((GROUPS, SPAN)),
            dma((2,)), dma((2,)),
            dma((GROUPS, SPAN)), dma((GROUPS, SPAN)),
            dma((GROUPS, SPAN)), dma((GROUPS, SPAN)),
            dma((HEADS,)), dma((HEADS,)),
            dma((GROUPS,)), dma((GROUPS,)),
        ],
        compiler_params=pltpu.CompilerParams(collective_id=0, has_side_effects=True),
    )(queries, keys, values, taps, mix_weight, docs)


def solution(mesh):
    placed = (
        P(("ba", "qb", "kb"), None),
        P(("ba", "kb"), None),
        P(("ba", "kb"), None),
        P(),
        P(),
        P("ba"),
    )
    return jax.shard_map(
        body, mesh=mesh, in_specs=placed, out_specs=P(("ba", "qb", "kb"), None), check_vma=False
    )
```
